768 devices in a mesh: dom: 96 (over x, z, core), sub: 8 (over y).
Axes of the slice: x: 4, y: 8, z: 12, core: 2. Of those that a mesh axis runs over, the one named last changes fastest.
Arguments:
- adjoint_field: float32 [98304, 5, 512], P(('dom', 'sub')), may hold values from -6 to 6
- metric: float32 [98304, 3, 512], P(('dom', 'sub')), may hold values from 0.5 to 4
- velocity: float32 [98304, 3, 512], P(('dom', 'sub')), may hold values from -2 to 2
- mortar_route: int32 [98304, 1], P(('dom', 'sub')), may hold values from 0 to 95, as said below
- mortar_element: int32 [98304, 1], P(('dom', 'sub')), may hold values from 0 to 127
- face_code: int32 [98304, 1], P(('dom', 'sub')), may hold values from 0 to 7
- hanging: int32 [98304, 1], P(('dom', 'sub')), may hold values 0 or 1
Outputs:
- result: float32 [98304, 5, 512], P(('dom', 'sub'))
The draws below stay inside these ranges and needn't reach their ends.
Inputs may be any that keep to these rules, and one draw needn't show every extreme that they name: `mortar_route`: each element's value is its own device's dom index d or one of d - 2, d - 1, d + 1, d + 2 taken modulo 96. In each aligned block of 128 rows (the elements of one device) no value is named by more than 96 rows, and some value by exactly 96.
All inputs are finite; a program needn't handle non-finite values. No bound on the sum of `hanging` on one device may be relied on, other than what follows from the above.
Results may differ from the reference program's by a relative error of at most 0.00088.
Values may be sent and summed in bfloat16 or wider, within the bound.
A program may use at most 32 MiB of HBM per device.

```python
import math
import jax
import jax.numpy as jnp
import numpy as np
from jax import lax

NODES = 8
FIELDS = 5
E_DEV = 128
CAP = 96
ELEMS = 98304
N_DOM = 96
N_SUB = 8


def route_block(key, dom_index):
    keys = jax.random.split(key, 5)
    rest = E_DEV - CAP
    first = jax.random.randint(keys[0], (), max(0, rest - 3 * CAP), min(CAP, rest) + 1)
    left_one = rest - first
    second = jax.random.randint(keys[1], (), jnp.maximum(0, left_one - 2 * CAP), jnp.minimum(CAP, left_one) + 1)
    left_two = left_one - second
    third = jax.random.randint(keys[2], (), jnp.maximum(0, left_two - CAP), jnp.minimum(CAP, left_two) + 1)
    fourth = left_two - third
    counts = jnp.stack([jnp.array(CAP, jnp.int32), first.astype(jnp.int32), second.astype(jnp.int32), third.astype(jnp.int32), fourth.astype(jnp.int32)])
    ends = jnp.cumsum(counts)
    labels = jax.random.permutation(keys[3], 5).astype(jnp.int32) - 2
    positions = jnp.arange(E_DEV, dtype=jnp.int32)
    group = jnp.sum((positions[:, None] >= ends[None, :]).astype(jnp.int32), axis=1)
    values = (dom_index + labels[group] + N_DOM) % N_DOM
    order = jax.random.permutation(keys[4], E_DEV)
    return jnp.zeros((E_DEV,), jnp.int32).at[order].set(values.astype(jnp.int32))


def draw_mortar_route(key, part):
    blocks = ELEMS // E_DEV
    keys = jax.random.split(jax.random.fold_in(key, 7), blocks)
    dom_ids = (jnp.arange(blocks, dtype=jnp.int32) // N_SUB).astype(jnp.int32)
    routes = jax.vmap(route_block)(keys, dom_ids)
    return routes.reshape(ELEMS, 1).astype(jnp.int32)


def touch_ends(values, key, smallest, high):
    longest = values.shape.index(max(values.shape))
    spots = []
    for shift in (0, 1):
        where = [jax.random.randint(jax.random.fold_in(key, axis), (), 0, length) for axis, length in enumerate(values.shape)]
        where[longest] = (where[longest] + shift) % values.shape[longest]
        spots.append(tuple(where))
    return values.at[spots[0]].set(smallest).at[spots[1]].set(high)


def block_levels(rng, dims, shards, low, top_value):
    factor_of = 1.0
    for dim, parts in shards:
        heights = jax.random.uniform(jax.random.fold_in(jax.random.fold_in(rng, 6), dim), (parts,), jnp.float32, low / len(shards), top_value / len(shards))
        factor_of = factor_of * jnp.repeat(jnp.exp(heights), dims[dim] // parts).reshape((-1,) + (1,) * (len(dims) - 1 - dim))
    return factor_of


def bell_draw(key, shape, deviation, limit, cuts=(), held_as=jnp.bfloat16):
    entries = jax.random.normal(key, shape, jnp.float32) * deviation
    if len(cuts) > 0:
        entries = block_levels(key, shape, cuts, -0.22, 0.18) * entries
    return jnp.clip(entries, min=-limit, max=limit).astype(held_as)


def setup_inputs(seed: int = 0) -> dict:
    streams_of = jax.random.split(jax.random.key(seed), 8)
    adjoint_field = bell_draw(streams_of[0], (ELEMS, FIELDS, NODES ** 3), 1.0, 6.0, ((0, 768),), jnp.float32)
    metric = jnp.clip(jnp.exp(math.log(4.0) - 2.0794415 * jax.random.uniform(streams_of[1], (ELEMS, 3, NODES ** 3), jnp.float32) ** block_levels(streams_of[1], (ELEMS, 3, NODES ** 3), ((0, 768),), -0.2, 0.2)), 0.5, 4.0)
    velocity = bell_draw(streams_of[2], (ELEMS, 3, NODES ** 3), 0.3, 2.0, ((0, 768),), jnp.float32)
    mortar_route = draw_mortar_route(jax.random.fold_in(streams_of[7], 71), 0)
    mortar_element = touch_ends(jax.random.randint(streams_of[4], (ELEMS, 1), 0, E_DEV), jax.random.fold_in(streams_of[4], 1), 0, E_DEV - 1).astype(jnp.int32)
    face_code = touch_ends(jax.random.randint(streams_of[5], (ELEMS, 1), 0, 8), jax.random.fold_in(streams_of[5], 1), 0, 7).astype(jnp.int32)
    hanging = touch_ends((jax.random.randint(streams_of[6], (ELEMS, 1), 0, 4) < 3).astype(jnp.int32), jax.random.fold_in(streams_of[6], 1), 0, 1)
    return {"adjoint_field": adjoint_field, "metric": metric, "velocity": velocity, "mortar_route": mortar_route, "mortar_element": mortar_element, "face_code": face_code, "hanging": hanging}


gll_nodes = np.array([-1.0, -0.8717401485096066, -0.5917001814331423, -0.2092992179024789, 0.2092992179024789, 0.5917001814331423, 0.8717401485096066, 1.0])
viscosity = 0.005


def legendre_seven(points):
    prev = np.ones(points.shape)
    curr = np.array(points)
    for order in range(1, 7):
        nxt = ((2 * order + 1) * points * curr - order * prev) / (order + 1)
        prev, curr = curr, nxt
    return curr


def diff_matrix():
    values = legendre_seven(gll_nodes)
    result_mat = np.zeros((8, 8))
    for row in range(8):
        for col in range(8):
            if row != col:
                result_mat[row, col] = values[row] / (values[col] * (gll_nodes[row] - gll_nodes[col]))
    result_mat[0, 0] = -14.0
    result_mat[7, 7] = 14.0
    return result_mat


def lagrange_at(points):
    basis = np.ones((8, 8))
    for row in range(8):
        for col in range(8):
            for other in range(8):
                if other != col:
                    basis[row, col] *= (points[row] - gll_nodes[other]) / (gll_nodes[col] - gll_nodes[other])
    return basis


def face_tables():
    halves = [lagrange_at((gll_nodes - 1.0) / 2.0), lagrange_at((gll_nodes + 1.0) / 2.0)]
    perm_mat = np.zeros((64, 64))
    for col in range(64):
        perm_mat[(col % 8) * 8 + col // 8, col] = 1.0
    tables = []
    for code in range(8):
        mat = np.kron(halves[code % 2], halves[(code // 2) % 2])
        if code >= 4:
            mat = mat @ perm_mat
        tables.append(mat)
    return np.stack(tables).astype(np.float32)


def kron_tables():
    dmat = diff_matrix()
    eye_eight = np.eye(8)
    first = np.kron(np.kron(eye_eight, dmat), eye_eight)
    second = np.kron(np.kron(eye_eight, eye_eight), dmat)
    return dmat.astype(np.float32), first.astype(np.float32), second.astype(np.float32)


def fold_faces(fine, codes):
    tables = jnp.asarray(face_tables())
    total = jnp.zeros(fine.shape, jnp.float32)
    for code in range(8):
        mapped = jnp.einsum("efa,ab->efb", fine, tables[code], precision=lax.Precision.HIGHEST)
        total = total + jnp.where((codes == code)[:, :, None], mapped, 0.0)
    return total


def derive(field, dim, mats):
    dmat, first, second = mats
    count = field.shape[0]
    if dim == 0:
        cube = field.reshape(count, 5, 8, 64)
        return jnp.einsum("ai,efip->efap", dmat, cube, precision=lax.Precision.HIGHEST).reshape(count, 5, 512)
    kron_mat = first if dim == 1 else second
    return jnp.einsum("efp,qp->efq", field, kron_mat, precision=lax.Precision.HIGHEST)


def derive_back(field, dim, mats):
    dmat, first, second = mats
    count = field.shape[0]
    if dim == 0:
        cube = field.reshape(count, 5, 8, 64)
        return jnp.einsum("ai,efap->efip", dmat, cube, precision=lax.Precision.HIGHEST).reshape(count, 5, 512)
    kron_mat = first if dim == 1 else second
    return jnp.einsum("efq,qp->efp", field, kron_mat, precision=lax.Precision.HIGHEST)


def apply_adjoint(summed, metric, velocity):
    mats = tuple(jnp.asarray(m) for m in kron_tables())
    total = jnp.zeros(summed.shape, jnp.float32)
    for dim in range(3):
        inner = viscosity * metric[:, dim:dim + 1] * derive(summed, dim, mats) + velocity[:, dim:dim + 1] * summed
        total = total + derive_back(inner, dim, mats)
    return total


def reference(adjoint_field, metric, velocity, mortar_route, mortar_element, face_code, hanging):
    count = adjoint_field.shape[0]
    field_cube = adjoint_field.reshape(count, 5, 8, 8, 8)
    fine = field_cube[:, :, :, 7, :].reshape(count, 5, 64)
    hang_f = hanging.astype(jnp.float32)
    folded = (fold_faces(fine, face_code) * hang_f[:, :, None]).astype(jnp.bfloat16)
    element_ids = jnp.arange(count, dtype=jnp.int32)
    sub_index = (element_ids // E_DEV) % N_SUB
    target = ((mortar_route[:, 0] * N_SUB + sub_index) * E_DEV + mortar_element[:, 0]).astype(jnp.int32)
    mortar = jnp.zeros((count, 5, 64), jnp.float32).at[target].add(folded.astype(jnp.float32))
    keep = (1.0 - hang_f)[:, :, None, None]
    field_cube = field_cube.at[:, :, :, 7, :].set(field_cube[:, :, :, 7, :] * keep)
    field_cube = field_cube.at[:, :, :, 0, :].add(mortar.reshape(count, 5, 8, 8))
    shared = field_cube[:-1, :, 7] + field_cube[1:, :, 0]
    field_cube = field_cube.at[:-1, :, 7].set(shared).at[1:, :, 0].set(shared)
    summed = field_cube.reshape(count // E_DEV, E_DEV, 5, 512)
    metric_b = metric.reshape(count // E_DEV, E_DEV, 3, 512)
    velocity_b = velocity.reshape(count // E_DEV, E_DEV, 3, 512)
    result = lax.map(lambda t: apply_adjoint(t[0], t[1], t[2]), (summed, metric_b, velocity_b))
    return result.reshape(count, 5, 512)
```

```python
import functools

import jax
import jax.numpy as jnp
import ml_dtypes
import numpy as np
from jax import lax
from jax.experimental import pallas as pl
from jax.experimental.pallas import tpu as pltpu
from jax.sharding import PartitionSpec as P

gll_nodes = np.array(
    [
        -1.0,
        -0.8717401485096066,
        -0.5917001814331423,
        -0.2092992179024789,
        0.2092992179024789,
        0.5917001814331423,
        0.8717401485096066,
        1.0,
    ]
)
viscosity = 0.005
OFFSETS = (-2, -1, 1, 2)
BF = jnp.bfloat16
F32 = jnp.float32


def legendre_seven(points):
    prev = np.ones(points.shape)
    curr = np.array(points)
    for order in range(1, 7):
        nxt = ((2 * order + 1) * points * curr - order * prev) / (order + 1)
        prev, curr = (curr, nxt)
    return curr


def diff_matrix():
    values = legendre_seven(gll_nodes)
    mat = np.zeros((8, 8))
    for row in range(8):
        for col in range(8):
            if row != col:
                mat[row, col] = values[row] / (values[col] * (gll_nodes[row] - gll_nodes[col]))
    mat[0, 0] = -14.0
    mat[7, 7] = 14.0
    return mat


def lagrange_at(points):
    basis = np.ones((8, 8))
    for row in range(8):
        for col in range(8):
            for other in range(8):
                if other != col:
                    basis[row, col] *= (points[row] - gll_nodes[other]) / (
                        gll_nodes[col] - gll_nodes[other]
                    )
    return basis


def split(mat):
    mat = np.asarray(mat, np.float32)
    high = mat.astype(ml_dtypes.bfloat16)
    low = (mat - high.astype(np.float32)).astype(ml_dtypes.bfloat16)
    return np.stack([high, low])


def fold_table():
    halves = [lagrange_at((gll_nodes - 1.0) / 2.0), lagrange_at((gll_nodes + 1.0) / 2.0)]
    table = np.zeros((8, 8, 8, 4, 64))
    for code in range(4):
        mat = np.kron(halves[code % 2], halves[code // 2]).astype(np.float32)
        table[:, 7, :, code, :] = mat.reshape(8, 8, 64)
    return split(table.reshape(512, 256))


def turn_table():
    table = np.zeros((2, 64, 2, 2, 64), np.float32)
    for node in range(64):
        table[:, node, 0, :, node] = 1.0
        table[:, (node % 8) * 8 + node // 8, 1, :, node] = 1.0
    return table.reshape(128, 256).astype(ml_dtypes.bfloat16)


def spread_table():
    table = np.zeros((2, 2, 2, 64, 8, 8, 8), np.float32)
    for half in range(2):
        for node in range(64):
            table[half, :, half, node, node // 8, 0, node % 8] = 1.0
    return table.reshape(2, 256, 512).astype(ml_dtypes.bfloat16)


def derivative_tables():
    dmat = diff_matrix().astype(np.float32)
    eye = np.eye(8)
    along_i = np.kron(np.kron(dmat, eye), eye).T
    along_j = np.kron(np.kron(np.eye(4), dmat), eye).T
    along_k = np.kron(np.kron(np.eye(4), eye), dmat).T
    return split(along_i), np.stack([split(along_j), split(along_k)])


def halves_of(value):
    high = value.astype(BF)
    low = (value - high.astype(F32)).astype(BF)
    return high, low


def mm(a, b):
    return jnp.dot(a, b, preferred_element_type=F32)


def mmt(a, b):
    return lax.dot_general(a, b, (((1,), (1,)), ((), ())), preferred_element_type=F32)


ROWS = 336


def exchange_kernel(
    n_dom,
    n_sub,
    x_ref,
    route_ref,
    elem_ref,
    code_ref,
    hang_ref,
    fold_ref,
    turn_ref,
    spread_ref,
    out_ref,
    send,
    got,
    low_send,
    high_send,
    edge_got,
    low_pad,
    high_pad,
    send_sem,
    recv_sem,
    edge_send_sem,
    edge_recv_sem,
):
    dom = lax.axis_index("dom")
    sub = lax.axis_index("sub")
    peers = [{"dom": lax.rem(dom + o + n_dom, n_dom), "sub": sub} for o in OFFSETS]
    place = dom * n_sub + sub
    total = n_dom * n_sub
    before = lax.rem(place + total - 1, total)
    after = lax.rem(place + 1, total)
    prev_dev = {"dom": before // n_sub, "sub": lax.rem(before, n_sub)}
    next_dev = {"dom": after // n_sub, "sub": lax.rem(after, n_sub)}

    barrier = pltpu.get_barrier_semaphore()
    for dev in peers + [prev_dev, next_dev]:
        pl.semaphore_signal(barrier, inc=1, device_id=dev, device_id_type=pl.DeviceIdType.MESH)

    lane = lax.broadcasted_iota(jnp.int32, (128, 128), 1)
    row = lax.broadcasted_iota(jnp.int32, (128, 128), 0)
    left = lane < 64

    def column(ref):
        return jnp.broadcast_to(ref[...].astype(F32), (128, 128)).T

    code = column(code_ref).astype(jnp.int32)
    hang = column(hang_ref)
    quarter = lax.rem(code, 4)
    in_first = quarter < 2
    wanted = jnp.where((lax.rem(quarter, 2) == 0) == left, hang, 0.0)
    turned = code >= 4

    faces = []
    for f in range(5):
        high, low = halves_of(x_ref[f])
        mapped = mm(high, fold_ref[0]) + mm(low, fold_ref[0]) + mm(high, fold_ref[1])
        picked = jnp.where(in_first, mapped[:, :128], mapped[:, 128:]) * wanted
        both = mm(picked.astype(BF), turn_ref[...])
        faces.append(jnp.where(turned, both[:, 128:], both[:, :128]))
    send[0:128, :] = jnp.where(left, faces[0], faces[1]).astype(BF)
    send[128:256, :] = jnp.where(left, faces[2], faces[3]).astype(BF)
    send[256:320, :] = jnp.where(left[:64], faces[4][:64], faces[4][64:]).astype(BF)
    meta_row = lax.broadcasted_iota(jnp.int32, (16, 128), 0)
    send[320:336, :] = jnp.where(
        meta_row == 0,
        jnp.broadcast_to(route_ref[...].astype(F32), (16, 128)),
        jnp.broadcast_to(elem_ref[...].astype(F32), (16, 128)),
    ).astype(BF)

    pl.semaphore_wait(barrier, 6)
    copies = []
    for n, dev in enumerate(peers):
        copy = pltpu.make_async_remote_copy(
            src_ref=send,
            dst_ref=got.at[n],
            send_sem=send_sem.at[n],
            recv_sem=recv_sem.at[n],
            device_id=dev,
            device_id_type=pl.DeviceIdType.MESH,
        )
        copy.start()
        copies.append(copy)

    def absorb(total, block):
        route = block[320:321, :].astype(F32)
        elem = block[321:322, :].astype(F32)
        dest = jnp.where(route == dom.astype(F32), elem, -1.0)
        hit = (jnp.broadcast_to(dest, (128, 128)) == row.astype(F32)).astype(F32).astype(BF)
        tail = block[256:320, :].astype(F32)
        last = jnp.concatenate(
            [jnp.where(left[:64], tail, 0.0), jnp.where(left[:64], 0.0, tail)], axis=0
        ).astype(BF)
        return [
            total[0] + mm(hit, block[0:128, :]),
            total[1] + mm(hit, block[128:256, :]),
            total[2] + mm(hit, last),
        ]

    sums = absorb([jnp.zeros((128, 128), F32)] * 3, send)
    for n, copy in enumerate(copies):
        copy.wait_recv()
        sums = absorb(sums, got.at[n])

    wide_lane = lax.broadcasted_iota(jnp.int32, (128, 512), 1)
    loses = lax.rem(wide_lane, 64) >= 56
    keep = 1.0 - hang
    keep = jnp.where(loses, jnp.concatenate([keep] * 4, axis=1), 1.0)
    packed = []
    for part in sums:
        high, low = halves_of(part)
        packed.append(jnp.concatenate([high, low], axis=1))
    for f in range(5):
        spread = mm(packed[f // 2], spread_ref[f % 2])
        if f == 4:
            spread = spread + mm(packed[2], spread_ref[1])
        value = x_ref[f] * keep + spread
        out_ref[f, :, 128:384] = value[:, 128:384]
        low_pad[f, 8:136, :] = value[:, 0:128]
        high_pad[f, 8:136, :] = value[:, 384:512]
        low_send[f : f + 1, :] = value[0:1, 0:128]
        high_send[f : f + 1, :] = value[127:128, 384:512]

    to_prev = pltpu.make_async_remote_copy(
        src_ref=low_send,
        dst_ref=edge_got.at[0],
        send_sem=edge_send_sem.at[0],
        recv_sem=edge_recv_sem.at[0],
        device_id=prev_dev,
        device_id_type=pl.DeviceIdType.MESH,
    )
    to_prev.start()
    to_next = pltpu.make_async_remote_copy(
        src_ref=high_send,
        dst_ref=edge_got.at[1],
        send_sem=edge_send_sem.at[1],
        recv_sem=edge_recv_sem.at[1],
        device_id=next_dev,
        device_id_type=pl.DeviceIdType.MESH,
    )
    to_next.start()
    to_prev.wait_recv()
    to_next.wait_recv()
    has_next = jnp.where(place < total - 1, 1.0, 0.0)
    has_prev = jnp.where(place > 0, 1.0, 0.0)
    for f in range(5):
        low_pad[f, 136:137, :] = edge_got[0, f : f + 1, :] * has_next
        high_pad[f, 7:8, :] = edge_got[1, f : f + 1, :] * has_prev
        above = low_pad[f, 9:137, :]
        below = high_pad[f, 7:135, :]
        out_ref[f, :, 0:128] = low_pad[f, 8:136, :] + jnp.where(
            left, pltpu.roll(below, 64, 1), 0.0
        )
        out_ref[f, :, 384:512] = high_pad[f, 8:136, :] + jnp.where(
            left, 0.0, pltpu.roll(above, 64, 1)
        )
    for copy in copies:
        copy.wait_send()
    to_prev.wait_send()
    to_next.wait_send()


def operator_kernel(u_ref, metric_ref, velocity_ref, i_ref, jk_ref, out_ref):
    u = u_ref[...].reshape(640, 512)
    high, low = halves_of(u)
    pieces = [slice(0, 256), slice(256, 512)]

    def inner(dim, cols, derived):
        m = metric_ref[dim, :, cols] * viscosity
        v = velocity_ref[dim, :, cols]
        cube = derived.reshape(5, 128, 256)
        value = cube * m[None] + u_ref[:, :, cols] * v[None]
        return halves_of(value.reshape(640, 256))

    parts_i = []
    for cols in pieces:
        derived = jnp.zeros((640, 256), F32)
        for rows in pieces:
            derived += mm(high[:, rows], i_ref[0, rows, cols])
            derived += mm(low[:, rows], i_ref[0, rows, cols])
            derived += mm(high[:, rows], i_ref[1, rows, cols])
        parts_i.append(inner(0, cols, derived))
    for n, cols in enumerate(pieces):
        total = jnp.zeros((640, 256), F32)
        for m, rows in enumerate(pieces):
            a, b = parts_i[m]
            total += mmt(a, i_ref[0, cols, rows])
            total += mmt(b, i_ref[0, cols, rows])
            total += mmt(a, i_ref[1, cols, rows])
        for dim in (1, 2):
            derived = mm(high[:, cols], jk_ref[dim - 1, 0])
            derived += mm(low[:, cols], jk_ref[dim - 1, 0])
            derived += mm(high[:, cols], jk_ref[dim - 1, 1])
            a, b = inner(dim, cols, derived)
            total += mmt(a, jk_ref[dim - 1, 0])
            total += mmt(b, jk_ref[dim - 1, 0])
            total += mmt(a, jk_ref[dim - 1, 1])
        out_ref[:, :, cols] = total.reshape(5, 128, 256)


def shards(n_dom, n_sub, adjoint_field, metric, velocity, route, element, code, hanging):
    x = jnp.transpose(adjoint_field, (1, 0, 2))
    met = jnp.transpose(metric, (1, 0, 2))
    vel = jnp.transpose(velocity, (1, 0, 2))
    rows = [a.reshape(1, 128) for a in (route, element, code, hanging)]
    along_i, along_jk = derivative_tables()
    vmem = pl.BlockSpec(memory_space=pltpu.VMEM)
    u = pl.pallas_call(
        functools.partial(exchange_kernel, n_dom, n_sub),
        out_shape=jax.ShapeDtypeStruct((5, 128, 512), F32),
        in_specs=[vmem] * 8,
        out_specs=vmem,
        scratch_shapes=[
            pltpu.VMEM((ROWS, 128), BF),
            pltpu.VMEM((4, ROWS, 128), BF),
            pltpu.VMEM((8, 128), F32),
            pltpu.VMEM((8, 128), F32),
            pltpu.VMEM((2, 8, 128), F32),
            pltpu.VMEM((5, 144, 128), F32),
            pltpu.VMEM((5, 144, 128), F32),
            pltpu.SemaphoreType.DMA((4,)),
            pltpu.SemaphoreType.DMA((4,)),
            pltpu.SemaphoreType.DMA((2,)),
            pltpu.SemaphoreType.DMA((2,)),
        ],
        compiler_params=pltpu.CompilerParams(
            collective_id=0, has_side_effects=True, vmem_limit_bytes=24 << 20
        ),
        name="exchange",
    )(x, *rows, jnp.asarray(fold_table()), jnp.asarray(turn_table()), jnp.asarray(spread_table()))
    result = pl.pallas_call(
        operator_kernel,
        out_shape=jax.ShapeDtypeStruct((5, 128, 512), F32),
        in_specs=[vmem] * 5,
        out_specs=vmem,
        compiler_params=pltpu.CompilerParams(vmem_limit_bytes=40 << 20),
        name="operator",
    )(u, met, vel, jnp.asarray(along_i), jnp.asarray(along_jk))
    return jnp.transpose(result, (1, 0, 2))


def solution(mesh):
    sizes = dict(zip(mesh.axis_names, mesh.devices.shape))
    block = P(("dom", "sub"), None, None)
    flat = P(("dom", "sub"), None)
    return jax.shard_map(
        functools.partial(shards, sizes["dom"], sizes["sub"]),
        mesh=mesh,
        in_specs=(block, block, block, flat, flat, flat, flat),
        out_specs=block,
        check_vma=False,
    )
```

```python
import functools

import jax
import jax.numpy as jnp
import ml_dtypes
import numpy as np
from jax import lax
from jax.experimental import pallas as pl
from jax.experimental.pallas import tpu as pltpu
from jax.sharding import PartitionSpec as P

gll_nodes = np.array(
    [
        -1.0,
        -0.8717401485096066,
        -0.5917001814331423,
        -0.2092992179024789,
        0.2092992179024789,
        0.5917001814331423,
        0.8717401485096066,
        1.0,
    ]
)
viscosity = 0.005
OFFSETS = (-2, -1, 1, 2)
BF = jnp.bfloat16
F32 = jnp.float32


def legendre_seven(points):
    prev = np.ones(points.shape)
    curr = np.array(points)
    for order in range(1, 7):
        nxt = ((2 * order + 1) * points * curr - order * prev) / (order + 1)
        prev, curr = (curr, nxt)
    return curr


def diff_matrix():
    values = legendre_seven(gll_nodes)
    mat = np.zeros((8, 8))
    for row in range(8):
        for col in range(8):
            if row != col:
                mat[row, col] = values[row] / (values[col] * (gll_nodes[row] - gll_nodes[col]))
    mat[0, 0] = -14.0
    mat[7, 7] = 14.0
    return mat


def lagrange_at(points):
    basis = np.ones((8, 8))
    for row in range(8):
        for col in range(8):
            for other in range(8):
                if other != col:
                    basis[row, col] *= (points[row] - gll_nodes[other]) / (
                        gll_nodes[col] - gll_nodes[other]
                    )
    return basis


def split(mat):
    mat = np.asarray(mat, np.float32)
    high = mat.astype(ml_dtypes.bfloat16)
    low = (mat - high.astype(np.float32)).astype(ml_dtypes.bfloat16)
    return np.stack([high, low])


def fold_table():
    parts = [lagrange_at((gll_nodes - 1.0) / 2.0), lagrange_at((gll_nodes + 1.0) / 2.0)]
    turn = np.zeros((64, 64))
    for col in range(64):
        turn[col % 8 * 8 + col // 8, col] = 1.0
    mats = []
    for code in range(8):
        mat = np.kron(parts[code % 2], parts[code // 2 % 2])
        mats.append(mat @ turn if code >= 4 else mat)
    high, low = split(np.stack(mats, axis=1))
    table = np.zeros((2, 2, 8, 8, 8, 64), np.float32)
    for i in range(8):
        a, b = divmod(i, 2)
        rows = slice(8 * i, 8 * i + 8)
        table[0, b, 7 - a] = high[rows].astype(np.float32)
        table[0, b, 3 - a] = high[rows].astype(np.float32)
        table[1, b, 7 - a] = low[rows].astype(np.float32)
    return table.reshape(256, 512).astype(ml_dtypes.bfloat16)


def face_derivatives(dmat):
    eye = np.eye(8)
    return np.kron(dmat, eye).T, np.kron(eye, dmat).T


def to_low_face():
    table = np.zeros((8, 8, 8, 8, 8))
    for i in range(8):
        for k in range(8):
            table[i, k, i, 0, k] = 1.0
    return table.reshape(64, 512)


def tables():
    dmat = diff_matrix().astype(np.float32)
    eye = np.eye(8)
    along_i = np.kron(np.kron(dmat, eye), eye).T
    along_j = np.kron(np.kron(np.eye(4), dmat), eye).T
    along_k = np.kron(np.kron(np.eye(4), eye), dmat).T
    i_tab = split(along_i)
    jk_tab = np.stack([split(along_j), split(along_k)])

    first, second = face_derivatives(dmat)
    both = np.concatenate([first, second], axis=1)
    zero = np.zeros((64, 128))
    high, low = [t.astype(np.float32) for t in split(both)]
    pair_high = np.block([[high, zero], [zero, high]])
    pair_low = np.block([[low, zero], [zero, low]])
    forward = np.stack(
        [np.concatenate([pair_high, pair_high]), np.concatenate([pair_low, 0 * pair_low])]
    )
    single = np.concatenate([high, low, high, 0 * high])
    back = both.T
    spread = to_low_face()
    bh, bl = [t.astype(np.float32) for t in split(back)]
    down = np.stack(
        [np.concatenate([bh, bh]) @ spread, np.concatenate([bl, 0 * bl]) @ spread]
    )
    twice = np.concatenate([np.eye(64), np.eye(64)], axis=1)
    single_back = np.stack(
        [np.concatenate([bh, bh]) @ twice, np.concatenate([bl, 0 * bl]) @ twice]
    )
    every = np.zeros((8, 8, 8, 8, 8))
    for i in range(8):
        for k in range(8):
            every[i, k, i, :, k] = 1.0
    every = every.reshape(64, 512)
    none = np.zeros((64, 512))
    expand = np.stack(
        [
            np.concatenate([every, none, every, none]),
            np.concatenate([none, every, none, every]),
        ]
    )
    gather = spread.T
    blank = np.zeros((512, 64))
    pick = np.concatenate([gather, blank, blank, gather], axis=1)
    cast = lambda t: np.asarray(t, np.float32).astype(ml_dtypes.bfloat16)
    vecs = np.zeros((8, 8, 8, 8), np.float32)
    vecs[0] = dmat[:, 0][None, :, None]
    vecs[1] = dmat[:, 0][:, None, None]
    vecs[2] = dmat[:, 7][:, None, None]
    late = np.concatenate(
        [expand[0], expand[1], down[0], down[1], forward[0], forward[1], single]
        + [single_back[0], single_back[1], np.zeros((256, 128))],
        axis=1,
    )
    return (
        fold_table(),
        i_tab,
        jk_tab,
        cast(pick),
        cast(late),
        vecs.reshape(8, 512),
    )


def halves_of(value):
    high = value.astype(BF)
    low = (value - high.astype(F32)).astype(BF)
    return high, low


def mm(a, b):
    return jnp.dot(a, b, preferred_element_type=F32)


def mmt(a, b):
    return lax.dot_general(a, b, (((1,), (1,)), ((), ())), preferred_element_type=F32)


def side_by_side(value):
    return jnp.concatenate(halves_of(value), axis=1)


ROWS = 336
HALF = [slice(0, 256), slice(256, 512)]
EXPAND, DOWN, FORWARD, SINGLE, SINGLE_BACK = 0, 1024, 2048, 2560, 2688


def apply_operator(x, met, vel, i_tab, jk_tab, out_ref):
    high, low = halves_of(x[...].reshape(640, 512))

    def inner(dim, cols, derived):
        m = met[dim, :, cols] * viscosity
        v = vel[dim, :, cols]
        value = derived.reshape(5, 128, 256) * m[None] + x[:, :, cols] * v[None]
        return halves_of(value.reshape(640, 256))

    parts_i = []
    for cols in HALF:
        derived = jnp.zeros((640, 256), F32)
        for rows in HALF:
            derived += mm(high[:, rows], i_tab[0, rows, cols])
            derived += mm(low[:, rows], i_tab[0, rows, cols])
            derived += mm(high[:, rows], i_tab[1, rows, cols])
        parts_i.append(inner(0, cols, derived))
    for cols in HALF:
        total = jnp.zeros((640, 256), F32)
        for m, rows in enumerate(HALF):
            a, b = parts_i[m]
            total += mmt(a, i_tab[0, cols, rows])
            total += mmt(b, i_tab[0, cols, rows])
            total += mmt(a, i_tab[1, cols, rows])
        for dim in (1, 2):
            derived = mm(high[:, cols], jk_tab[dim - 1, 0])
            derived += mm(low[:, cols], jk_tab[dim - 1, 0])
            derived += mm(high[:, cols], jk_tab[dim - 1, 1])
            a, b = inner(dim, cols, derived)
            total += mmt(a, jk_tab[dim - 1, 0])
            total += mmt(b, jk_tab[dim - 1, 0])
            total += mmt(a, jk_tab[dim - 1, 1])
        out_ref[:, :, cols] = total.reshape(5, 128, 256)


def kernel(n_dom, n_sub, *refs):
    (x_hbm, met_hbm, vel_hbm, route_hbm, elem_hbm, code_hbm, hang_hbm) = refs[:7]
    (fold_hbm, i_hbm, jk_hbm, pick_hbm, late_hbm, vecs_hbm) = refs[7:13]
    out_ref = refs[13]
    (x, met, vel, route_ref, elem_ref, code_ref, hang_ref) = refs[14:21]
    (fold, i_tab, jk_tab, pick, late, vecs) = refs[21:27]
    (send, got, low_send, high_send, edge_got, low_pad, high_pad, mortar_pad) = refs[27:35]
    (w_ref, face_met, face_vel, wi_ref, edge_met, edge_vel) = refs[35:41]
    (load_sem, send_sem, recv_sem, edge_send_sem, edge_recv_sem) = refs[41:46]

    dom = lax.axis_index("dom")
    sub = lax.axis_index("sub")
    mesh_id = pl.DeviceIdType.MESH
    peers = [{"dom": lax.rem(dom + o + n_dom, n_dom), "sub": sub} for o in OFFSETS]
    place = dom * n_sub + sub
    total = n_dom * n_sub
    before = lax.rem(place + total - 1, total)
    after = lax.rem(place + 1, total)
    prev_dev = {"dom": before // n_sub, "sub": lax.rem(before, n_sub)}
    next_dev = {"dom": after // n_sub, "sub": lax.rem(after, n_sub)}

    loads = []

    def load(src, dst):
        copy = pltpu.make_async_copy(src, dst, load_sem.at[len(loads)])
        copy.start()
        loads.append(copy)
        return copy

    x_loads = [load(x_hbm, x)]
    first_loads = [
        load(fold_hbm, fold),
        load(code_hbm, code_ref),
        load(hang_hbm, hang_ref),
        load(route_hbm, route_ref),
        load(elem_hbm, elem_ref),
    ]
    barrier = pltpu.get_barrier_semaphore()
    for dev in peers + [prev_dev, next_dev]:
        pl.semaphore_signal(barrier, inc=1, device_id=dev, device_id_type=mesh_id)
    later_loads = [
        load(i_hbm, i_tab),
        load(jk_hbm, jk_tab),
        load(met_hbm, met),
        load(vel_hbm, vel),
        load(pick_hbm, pick),
        load(late_hbm, late),
        load(vecs_hbm, vecs),
    ]

    lane = lax.broadcasted_iota(jnp.int32, (128, 128), 1)
    row = lax.broadcasted_iota(jnp.int32, (128, 128), 0)
    left = lane < 64
    slot = lax.rem(lane, 64) // 8

    low_send[...] = jnp.zeros((8, 128), F32)
    high_send[...] = jnp.zeros((8, 128), F32)
    for f in range(5):
        low_pad[f, 136:144, :] = jnp.zeros((8, 128), F32)
        high_pad[f, 0:8, :] = jnp.zeros((8, 128), F32)
    for c in range(3):
        mortar_pad[c, 0:8, :] = jnp.zeros((8, 128), F32)
        mortar_pad[c, 136:144, :] = jnp.zeros((8, 128), F32)

    for copy in first_loads:
        copy.wait()

    def column(ref):
        return jnp.broadcast_to(ref[...].astype(F32), (128, 128)).T

    code = column(code_ref).astype(jnp.int32)
    hang = column(hang_ref)
    odd = lax.rem(code, 2) == 1

    for copy in x_loads:
        copy.wait()
    faces = []
    for f in range(5):
        packed = jnp.where(
            slot == 7,
            x[f, :, 0:128],
            jnp.where(
                slot == 6,
                pltpu.roll(x[f, :, 128:256], 120, 1),
                jnp.where(
                    slot == 5,
                    pltpu.roll(x[f, :, 256:384], 112, 1),
                    pltpu.roll(x[f, :, 384:512], 104, 1),
                ),
            ),
        )
        high = packed.astype(BF)
        low = packed - high.astype(F32)
        mixed = jnp.where(slot >= 4, packed, pltpu.roll(low, 96, 1)).astype(BF)
        mapped = mm(jnp.concatenate([mixed, high], axis=1), fold[...])
        picked = jnp.where(
            code < 4,
            jnp.where(code < 2, mapped[:, 0:128], mapped[:, 128:256]),
            jnp.where(code < 6, mapped[:, 256:384], mapped[:, 384:512]),
        )
        picked = picked * hang
        other = pltpu.roll(picked, 64, 1)
        faces.append((jnp.where(odd, other, picked), jnp.where(odd, picked, other)))
    send[0:128, :] = jnp.where(left, faces[0][0], faces[1][1]).astype(BF)
    send[128:256, :] = jnp.where(left, faces[2][0], faces[3][1]).astype(BF)
    send[256:320, :] = jnp.where(left[:64], faces[4][0][:64], faces[4][1][64:]).astype(BF)
    meta_row = lax.broadcasted_iota(jnp.int32, (16, 128), 0)
    send[320:336, :] = jnp.where(
        meta_row == 0,
        jnp.broadcast_to(route_ref[...].astype(F32), (16, 128)),
        jnp.broadcast_to(elem_ref[...].astype(F32), (16, 128)),
    ).astype(BF)

    pl.semaphore_wait(barrier, 6)
    copies = []
    for n, dev in enumerate(peers):
        copy = pltpu.make_async_remote_copy(
            src_ref=send,
            dst_ref=got.at[n],
            send_sem=send_sem.at[n],
            recv_sem=recv_sem.at[n],
            device_id=dev,
            device_id_type=mesh_id,
        )
        copy.start()
        copies.append(copy)

    keep = 1.0 - hang
    keep = jnp.where(slot == 7, keep, 1.0)
    for f in range(5):
        x[f, :, 128:256] = x[f, :, 128:256] * keep
        x[f, :, 256:384] = x[f, :, 256:384] * keep
        low_pad[f, 8:136, :] = x[f, :, 0:128] * keep
        high_pad[f, 8:136, :] = x[f, :, 384:512] * keep
        above = low_pad[f, 9:137, :]
        below = high_pad[f, 7:135, :]
        x[f, :, 0:128] = low_pad[f, 8:136, :] + jnp.where(left, pltpu.roll(below, 64, 1), 0.0)
        x[f, :, 384:512] = high_pad[f, 8:136, :] + jnp.where(left, 0.0, pltpu.roll(above, 64, 1))
    for copy in later_loads:
        copy.wait()
    apply_operator(x, met, vel, i_tab, jk_tab, out_ref)

    wide = lax.broadcasted_iota(jnp.int32, (128, 512), 1)
    on_low = lax.rem(wide, 64) < 8
    weight = met[1] * viscosity * vecs[0:1, :] + jnp.where(on_low, vel[1], 0.0)
    wh, wl = halves_of(weight)
    for cols in HALF:
        w_ref[:, cols] = (
            mmt(wh[:, cols], jk_tab[0, 0])
            + mmt(wl[:, cols], jk_tab[0, 0])
            + mmt(wh[:, cols], jk_tab[0, 1])
        )

    def low_nodes(src):
        ah, al = halves_of(src[0])
        bh, bl = halves_of(src[2])
        return (
            mm(ah, pick[:, 0:128])
            + mm(al, pick[:, 0:128])
            + mm(bh, pick[:, 128:256])
            + mm(bl, pick[:, 128:256])
        )

    face_met[...] = low_nodes(met) * viscosity
    face_vel[...] = low_nodes(vel)

    edge_rows = lax.broadcasted_iota(jnp.int32, (16, 512), 0)
    edge_wide = lax.broadcasted_iota(jnp.int32, (16, 512), 1)
    head = edge_rows < 8

    def ends(src, dim):
        a = jnp.broadcast_to(src[dim, 0:1, :], (16, 512))
        b = jnp.broadcast_to(src[dim, 127:128, :], (16, 512))
        return a, b

    ma, mb = ends(met, 0)
    va, vb = ends(vel, 0)
    ea = ma * viscosity * vecs[1:2, :] + jnp.where(edge_wide < 64, va, 0.0)
    eb = mb * viscosity * vecs[2:3, :] + jnp.where(edge_wide >= 448, vb, 0.0)
    eh, el = halves_of(jnp.where(head, ea, eb))
    for cols in HALF:
        acc = jnp.zeros((16, 256), F32)
        for rows in HALF:
            acc += mmt(eh[:, rows], i_tab[0, cols, rows])
            acc += mmt(el[:, rows], i_tab[0, cols, rows])
            acc += mmt(eh[:, rows], i_tab[1, cols, rows])
        wi_ref[:, cols] = acc
    left16 = left[:16]
    head16 = row[:16] < 8

    def end_faces(src):
        j0, j7 = ends(src, 1)
        k0, k7 = ends(src, 2)
        a = jnp.where(left16, j0[:, 0:128], pltpu.roll(k0[:, 0:128], 64, 1))
        b = jnp.where(left16, pltpu.roll(j7[:, 384:512], 64, 1), k7[:, 384:512])
        return jnp.where(head16, a, b)

    edge_met[...] = end_faces(met) * viscosity
    edge_vel[...] = end_faces(vel)

    def absorb(sums, block):
        route = block[320:321, :].astype(F32)
        elem = block[321:322, :].astype(F32)
        dest = jnp.where(route == dom.astype(F32), elem, -1.0)
        hit = (jnp.broadcast_to(dest, (128, 128)) == row.astype(F32)).astype(F32).astype(BF)
        tail = block[256:320, :].astype(F32)
        last = jnp.concatenate(
            [jnp.where(left[:64], tail, 0.0), jnp.where(left[:64], 0.0, tail)], axis=0
        ).astype(BF)
        return [
            sums[0] + mm(hit, block[0:128, :]),
            sums[1] + mm(hit, block[128:256, :]),
            sums[2] + mm(hit, last),
        ]

    sums = absorb([jnp.zeros((128, 128), F32)] * 3, send)
    for n, copy in enumerate(copies):
        copy.wait_recv()
        sums = absorb(sums, got.at[n])
    sums[2] = sums[2] + pltpu.roll(sums[2], 64, 1)

    lane8 = lane[:8]
    for f in range(5):
        part = sums[f // 2]
        top, bottom = part[0:8, :], part[120:128, :]
        shift_low, shift_high = (64, 72) if f % 2 else (0, 8)
        if shift_low:
            top = pltpu.roll(top, shift_low, 1)
        bottom = pltpu.roll(bottom, shift_high, 1)
        top = jnp.where(lane8 < 8, top, 0.0)
        bottom = jnp.where((lane8 >= 64) & (lane8 < 72), bottom, 0.0)
        low_send[f : f + 1, :] = low_pad[f, 8:9, :] + top[0:1, :]
        high_send[f : f + 1, :] = high_pad[f, 135:136, :] + bottom[7:8, :]
    to_prev = pltpu.make_async_remote_copy(
        src_ref=low_send,
        dst_ref=edge_got.at[0],
        send_sem=edge_send_sem.at[0],
        recv_sem=edge_recv_sem.at[0],
        device_id=prev_dev,
        device_id_type=mesh_id,
    )
    to_prev.start()
    to_next = pltpu.make_async_remote_copy(
        src_ref=high_send,
        dst_ref=edge_got.at[1],
        send_sem=edge_send_sem.at[1],
        recv_sem=edge_recv_sem.at[1],
        device_id=next_dev,
        device_id_type=mesh_id,
    )
    to_next.start()

    node = lax.rem(lane, 64)
    for c in range(3):
        mortar_pad[c, 8:136, :] = sums[c]
    for c in range(3):
        above = mortar_pad[c, 9:137, :]
        below = mortar_pad[c, 7:135, :]
        shared = (
            sums[c]
            + jnp.where(node >= 56, pltpu.roll(above, 56, 1), 0.0)
            + jnp.where(node < 8, pltpu.roll(below, 72, 1), 0.0)
        )
        flipped = pltpu.roll(shared, 64, 1)
        pair = side_by_side(shared)
        slopes = mm(pair, late[:, FORWARD : FORWARD + 256]) + mm(
            pair, late[:, FORWARD + 256 : FORWARD + 512]
        )
        for g in range(2 if c < 2 else 1):
            f = 2 * c + g
            twice = jnp.where(left == (g == 0), shared, flipped)
            inner = face_met[...] * slopes[:, 128 * g : 128 * g + 128] + face_vel[...] * twice
            inner = side_by_side(inner)
            for n, cols in enumerate(HALF):
                at = 256 * n
                everywhere = mm(pair, late[:, EXPAND + 512 * g + at : EXPAND + 512 * g + at + 256])
                low_face = mm(inner, late[:, DOWN + at : DOWN + at + 256]) + mm(
                    inner, late[:, DOWN + 512 + at : DOWN + 512 + at + 256]
                )
                out_ref[f, :, cols] = out_ref[f, :, cols] + everywhere * w_ref[:, cols] + low_face

    to_prev.wait_recv()
    to_next.wait_recv()
    has_next = jnp.where(place < total - 1, 1.0, 0.0)
    has_prev = jnp.where(place > 0, 1.0, 0.0)
    from_next = edge_got[0] * has_next
    from_prev = edge_got[1] * has_prev
    face = jnp.concatenate(
        [
            jnp.where(left[:8], pltpu.roll(from_prev, 64, 1), from_prev),
            jnp.where(left[:8], from_next, pltpu.roll(from_next, 64, 1)),
        ],
        axis=0,
    )
    slope = mm(side_by_side(face), late[:, SINGLE : SINGLE + 128])
    inner = side_by_side(edge_met[...] * slope + edge_vel[...] * face)
    back = mm(inner, late[:, SINGLE_BACK : SINGLE_BACK + 128]) + mm(
        inner, late[:, SINGLE_BACK + 128 : SINGLE_BACK + 256]
    )
    part = jnp.concatenate([face] * 4, axis=1) * wi_ref[...]
    part = part + jnp.concatenate(
        [
            jnp.where(head16 & left16, back, 0.0),
            jnp.zeros((16, 256), F32),
            jnp.where(head16 | left16, 0.0, back),
        ],
        axis=1,
    )
    for f in range(5):
        out_ref[f, 0:1, :] = out_ref[f, 0:1, :] + part[f : f + 1, :]
        out_ref[f, 127:128, :] = out_ref[f, 127:128, :] + part[8 + f : 9 + f, :]

    for copy in copies:
        copy.wait_send()
    to_prev.wait_send()
    to_next.wait_send()


def shards(n_dom, n_sub, adjoint_field, metric, velocity, route, element, code, hanging):
    fields = [jnp.transpose(a, (1, 0, 2)) for a in (adjoint_field, metric, velocity)]
    rows = [a.reshape(1, 128) for a in (route, element, code, hanging)]
    consts = [jnp.asarray(t) for t in tables()]
    operands = [pltpu.with_memory_space_constraint(a, pltpu.HBM) for a in fields + rows + consts]
    result = pl.pallas_call(
        functools.partial(kernel, n_dom, n_sub),
        out_shape=pltpu.VMEM((5, 128, 512), F32),
        in_specs=[pl.BlockSpec(memory_space=pltpu.HBM)] * len(operands),
        out_specs=pl.BlockSpec(memory_space=pltpu.VMEM),
        scratch_shapes=[pltpu.VMEM(a.shape, a.dtype) for a in operands]
        + [
            pltpu.VMEM((ROWS, 128), BF),
            pltpu.VMEM((4, ROWS, 128), BF),
            pltpu.VMEM((8, 128), F32),
            pltpu.VMEM((8, 128), F32),
            pltpu.VMEM((2, 8, 128), F32),
            pltpu.VMEM((5, 144, 128), F32),
            pltpu.VMEM((5, 144, 128), F32),
            pltpu.VMEM((3, 144, 128), F32),
            pltpu.VMEM((128, 512), F32),
            pltpu.VMEM((128, 128), F32),
            pltpu.VMEM((128, 128), F32),
            pltpu.VMEM((16, 512), F32),
            pltpu.VMEM((16, 128), F32),
            pltpu.VMEM((16, 128), F32),
            pltpu.SemaphoreType.DMA((13,)),
            pltpu.SemaphoreType.DMA((4,)),
            pltpu.SemaphoreType.DMA((4,)),
            pltpu.SemaphoreType.DMA((2,)),
            pltpu.SemaphoreType.DMA((2,)),
        ],
        compiler_params=pltpu.CompilerParams(
            collective_id=0, has_side_effects=True, vmem_limit_bytes=40 << 20
        ),
        name="adjoint",
    )(*operands)
    return jnp.transpose(result, (1, 0, 2))


def solution(mesh):
    sizes = dict(zip(mesh.axis_names, mesh.devices.shape))
    block = P(("dom", "sub"), None, None)
    flat = P(("dom", "sub"), None)
    return jax.shard_map(
        functools.partial(shards, sizes["dom"], sizes["sub"]),
        mesh=mesh,
        in_specs=(block, block, block, flat, flat, flat, flat),
        out_specs=block,
        check_vma=False,
    )
```

```python
import functools

import jax
import jax.numpy as jnp
import ml_dtypes
import numpy as np
from jax import lax
from jax.experimental import pallas as pl
from jax.experimental.pallas import tpu as pltpu
from jax.sharding import PartitionSpec as P

gll_nodes = np.array(
    [
        -1.0,
        -0.8717401485096066,
        -0.5917001814331423,
        -0.2092992179024789,
        0.2092992179024789,
        0.5917001814331423,
        0.8717401485096066,
        1.0,
    ]
)
viscosity = 0.005
OFFSETS = (-2, -1, 1, 2)
BF = jnp.bfloat16
F32 = jnp.float32


def legendre_seven(points):
    prev = np.ones(points.shape)
    curr = np.array(points)
    for order in range(1, 7):
        nxt = ((2 * order + 1) * points * curr - order * prev) / (order + 1)
        prev, curr = (curr, nxt)
    return curr


def diff_matrix():
    values = legendre_seven(gll_nodes)
    mat = np.zeros((8, 8))
    for row in range(8):
        for col in range(8):
            if row != col:
                mat[row, col] = values[row] / (values[col] * (gll_nodes[row] - gll_nodes[col]))
    mat[0, 0] = -14.0
    mat[7, 7] = 14.0
    return mat


def lagrange_at(points):
    basis = np.ones((8, 8))
    for row in range(8):
        for col in range(8):
            for other in range(8):
                if other != col:
                    basis[row, col] *= (points[row] - gll_nodes[other]) / (
                        gll_nodes[col] - gll_nodes[other]
                    )
    return basis


def split(mat):
    mat = np.asarray(mat, np.float32)
    high = mat.astype(ml_dtypes.bfloat16)
    low = (mat - high.astype(np.float32)).astype(ml_dtypes.bfloat16)
    return np.stack([high, low])


def fold_table():
    parts = [lagrange_at((gll_nodes - 1.0) / 2.0), lagrange_at((gll_nodes + 1.0) / 2.0)]
    turn = np.zeros((64, 64))
    for col in range(64):
        turn[col % 8 * 8 + col // 8, col] = 1.0
    mats = []
    for code in range(8):
        mat = np.kron(parts[code % 2], parts[code // 2 % 2])
        mats.append(mat @ turn if code >= 4 else mat)
    high, low = split(np.stack(mats, axis=1))
    table = np.zeros((2, 2, 8, 8, 8, 64), np.float32)
    for i in range(8):
        a, b = divmod(i, 2)
        rows = slice(8 * i, 8 * i + 8)
        table[0, b, 7 - a] = high[rows].astype(np.float32)
        table[0, b, 3 - a] = high[rows].astype(np.float32)
        table[1, b, 7 - a] = low[rows].astype(np.float32)
    return table.reshape(256, 512).astype(ml_dtypes.bfloat16)


def face_derivatives(dmat):
    eye = np.eye(8)
    return np.kron(dmat, eye).T, np.kron(eye, dmat).T


def to_low_face():
    table = np.zeros((8, 8, 8, 8, 8))
    for i in range(8):
        for k in range(8):
            table[i, k, i, 0, k] = 1.0
    return table.reshape(64, 512)


def tables():
    dmat = diff_matrix().astype(np.float32)
    eye = np.eye(8)
    along_i = np.kron(np.kron(dmat, eye), eye).T
    along_j = np.kron(np.kron(np.eye(4), dmat), eye).T
    along_k = np.kron(np.kron(np.eye(4), eye), dmat).T
    i_tab = split(along_i)
    jk_tab = np.stack([split(along_j), split(along_k)])

    first, second = face_derivatives(dmat)
    both = np.concatenate([first, second], axis=1)
    zero = np.zeros((64, 128))
    high, low = [t.astype(np.float32) for t in split(both)]
    pair_high = np.block([[high, zero], [zero, high]])
    pair_low = np.block([[low, zero], [zero, low]])
    forward = np.stack(
        [np.concatenate([pair_high, pair_high]), np.concatenate([pair_low, 0 * pair_low])]
    )
    single = np.concatenate([high, low, high, 0 * high])
    back = both.T
    spread = to_low_face()
    bh, bl = [t.astype(np.float32) for t in split(back)]
    down = np.stack(
        [np.concatenate([bh, bh]) @ spread, np.concatenate([bl, 0 * bl]) @ spread]
    )
    twice = np.concatenate([np.eye(64), np.eye(64)], axis=1)
    single_back = np.stack(
        [np.concatenate([bh, bh]) @ twice, np.concatenate([bl, 0 * bl]) @ twice]
    )
    every = np.zeros((8, 8, 8, 8, 8))
    for i in range(8):
        for k in range(8):
            every[i, k, i, :, k] = 1.0
    every = every.reshape(64, 512)
    none = np.zeros((64, 512))
    expand = np.stack(
        [
            np.concatenate([every, none, every, none]),
            np.concatenate([none, every, none, every]),
        ]
    )
    gather = spread.T
    blank = np.zeros((512, 64))
    pick = np.concatenate([gather, blank, blank, gather], axis=1)
    cast = lambda t: np.asarray(t, np.float32).astype(ml_dtypes.bfloat16)
    vecs = np.zeros((8, 8, 8, 8), np.float32)
    vecs[0] = dmat[:, 0][None, :, None]
    vecs[1] = dmat[:, 0][:, None, None]
    vecs[2] = dmat[:, 7][:, None, None]
    late = np.concatenate(
        [expand[0], expand[1], down[0], down[1], forward[0], forward[1], single]
        + [single_back[0], single_back[1], np.zeros((256, 128))],
        axis=1,
    )
    return (
        fold_table(),
        i_tab,
        jk_tab,
        cast(pick),
        cast(late),
        vecs.reshape(8, 512),
    )


def halves_of(value):
    high = value.astype(BF)
    low = (value - high.astype(F32)).astype(BF)
    return high, low


def mm(a, b):
    return jnp.dot(a, b, preferred_element_type=F32)


def mmt(a, b):
    return lax.dot_general(a, b, (((1,), (1,)), ((), ())), preferred_element_type=F32)


def side_by_side(value):
    return jnp.concatenate(halves_of(value), axis=1)


ROWS = 336
HALF = [slice(0, 256), slice(256, 512)]
EXPAND, DOWN, FORWARD, SINGLE, SINGLE_BACK = 0, 1024, 2048, 2560, 2688


def apply_operator(x, met, vel, i_tab, jk_tab, out_ref):
    high, low = halves_of(x[...].reshape(640, 512))

    def inner(dim, cols, derived):
        m = met[dim, :, cols] * viscosity
        v = vel[dim, :, cols]
        value = derived.reshape(5, 128, 256) * m[None] + x[:, :, cols] * v[None]
        return halves_of(value.reshape(640, 256))

    parts_i = []
    for cols in HALF:
        derived = jnp.zeros((640, 256), F32)
        for rows in HALF:
            derived += mm(high[:, rows], i_tab[0, rows, cols])
            derived += mm(low[:, rows], i_tab[0, rows, cols])
            derived += mm(high[:, rows], i_tab[1, rows, cols])
        parts_i.append(inner(0, cols, derived))
    for cols in HALF:
        total = jnp.zeros((640, 256), F32)
        for m, rows in enumerate(HALF):
            a, b = parts_i[m]
            total += mmt(a, i_tab[0, cols, rows])
            total += mmt(b, i_tab[0, cols, rows])
            total += mmt(a, i_tab[1, cols, rows])
        for dim in (1, 2):
            derived = mm(high[:, cols], jk_tab[dim - 1, 0])
            derived += mm(low[:, cols], jk_tab[dim - 1, 0])
            derived += mm(high[:, cols], jk_tab[dim - 1, 1])
            a, b = inner(dim, cols, derived)
            total += mmt(a, jk_tab[dim - 1, 0])
            total += mmt(b, jk_tab[dim - 1, 0])
            total += mmt(a, jk_tab[dim - 1, 1])
        out_ref[:, :, cols] = total.reshape(5, 128, 256)


def kernel(n_dom, n_sub, *refs):
    (x_hbm, met_hbm, vel_hbm, route_hbm, elem_hbm, code_hbm, hang_hbm) = refs[:7]
    (fold_hbm, i_hbm, jk_hbm, pick_hbm, late_hbm, vecs_hbm) = refs[7:13]
    out_ref = refs[13]
    (x, met, vel, route_ref, elem_ref, code_ref, hang_ref) = refs[14:21]
    (fold, i_tab, jk_tab, pick, late, vecs) = refs[21:27]
    (send, got, edge_send, edge_got, edge_face, low_pad, high_pad, mortar_pad) = refs[27:35]
    (w_ref, face_met, face_vel, wi_ref, edge_met, edge_vel) = refs[35:41]
    (load_sem, send_sem, recv_sem, edge_send_sem, edge_recv_sem) = refs[41:46]

    dom = lax.axis_index("dom")
    sub = lax.axis_index("sub")
    mesh_id = pl.DeviceIdType.MESH
    peers = [{"dom": lax.rem(dom + o + n_dom, n_dom), "sub": sub} for o in OFFSETS]
    place = dom * n_sub + sub
    total = n_dom * n_sub

    def stepped(offset, step):
        at = lax.rem(dom + offset + n_dom, n_dom) * n_sub + sub
        at = lax.rem(at + step + total, total)
        return {"dom": at // n_sub, "sub": lax.rem(at, n_sub)}

    edge_peers = [stepped(o, 1) for o in range(-2, 3)] + [stepped(o, -1) for o in range(-2, 3)]

    loads = []

    def load(src, dst):
        copy = pltpu.make_async_copy(src, dst, load_sem.at[len(loads)])
        copy.start()
        loads.append(copy)
        return copy

    x_loads = []
    first_loads = [
        load(fold_hbm, fold),
        load(code_hbm, code_ref),
        load(hang_hbm, hang_ref),
        load(route_hbm, route_ref),
        load(elem_hbm, elem_ref),
    ]
    for f in range(5):
        x_loads.append(load(x_hbm.at[f], x.at[f]))
    barrier = pltpu.get_barrier_semaphore()
    for dev in peers + edge_peers:
        pl.semaphore_signal(barrier, inc=1, device_id=dev, device_id_type=mesh_id)
    later_loads = [
        load(i_hbm, i_tab),
        load(jk_hbm, jk_tab),
        load(met_hbm, met),
        load(vel_hbm, vel),
        load(pick_hbm, pick),
        load(late_hbm, late),
        load(vecs_hbm, vecs),
    ]

    lane = lax.broadcasted_iota(jnp.int32, (128, 128), 1)
    row = lax.broadcasted_iota(jnp.int32, (128, 128), 0)
    left = lane < 64
    slot = lax.rem(lane, 64) // 8

    for f in range(5):
        low_pad[f, 136:144, :] = jnp.zeros((8, 128), F32)
        high_pad[f, 0:8, :] = jnp.zeros((8, 128), F32)
    edge_face[...] = jnp.zeros((2, 8, 128), F32)
    for c in range(3):
        mortar_pad[c, 0:8, :] = jnp.zeros((8, 128), F32)
        mortar_pad[c, 136:144, :] = jnp.zeros((8, 128), F32)

    for copy in first_loads:
        copy.wait()

    def column(ref):
        return jnp.broadcast_to(ref[...].astype(F32), (128, 128)).T

    code = column(code_ref).astype(jnp.int32)
    hang = column(hang_ref)
    odd = lax.rem(code, 2) == 1

    keep = jnp.where(slot == 7, 1.0 - hang, 1.0)
    faces = []
    for f in range(5):
        x_loads[f].wait()
        packed = jnp.where(
            slot == 7,
            x[f, :, 0:128],
            jnp.where(
                slot == 6,
                pltpu.roll(x[f, :, 128:256], 120, 1),
                jnp.where(
                    slot == 5,
                    pltpu.roll(x[f, :, 256:384], 112, 1),
                    pltpu.roll(x[f, :, 384:512], 104, 1),
                ),
            ),
        )
        high = packed.astype(BF)
        low = packed - high.astype(F32)
        mixed = jnp.where(slot >= 4, packed, pltpu.roll(low, 96, 1)).astype(BF)
        mapped = mm(jnp.concatenate([mixed, high], axis=1), fold[...])
        picked = jnp.where(
            code < 4,
            jnp.where(code < 2, mapped[:, 0:128], mapped[:, 128:256]),
            jnp.where(code < 6, mapped[:, 256:384], mapped[:, 384:512]),
        )
        picked = picked * hang
        other = pltpu.roll(picked, 64, 1)
        faces.append((jnp.where(odd, other, picked), jnp.where(odd, picked, other)))
    pairs = [
        jnp.where(left, faces[0][0], faces[1][1]).astype(BF),
        jnp.where(left, faces[2][0], faces[3][1]).astype(BF),
        faces[4][0].astype(BF),
    ]
    edge_row = lax.broadcasted_iota(jnp.int32, (80, 128), 0)
    tile = edge_row // 8
    part = lax.rem(edge_row, 8)
    wanted_elem = jnp.where(tile < 5, 127, 0)
    wanted_dom = lax.rem(dom + lax.rem(tile, 5) - 2 + n_dom, n_dom)
    chosen = (jnp.broadcast_to(route_ref[...], (80, 128)) == wanted_dom) & (
        jnp.broadcast_to(elem_ref[...], (80, 128)) == wanted_elem
    )
    chosen = jnp.where(chosen, 1.0, 0.0)
    edge_sums = jnp.zeros((80, 128), F32)
    for c in range(3):
        edge_sums += mm(jnp.where(part == c, chosen, 0.0).astype(BF), pairs[c])
    edge_send[...] = edge_sums
    for f in range(5):
        edge_send[19 + f : 20 + f, :] = x[f, 127:128, 384:512] * keep[127:128, :]
        edge_send[59 + f : 60 + f, :] = x[f, 0:1, 0:128] * keep[0:1, :]
    send[0:128, :] = pairs[0]
    send[128:256, :] = pairs[1]
    send[256:320, :] = jnp.where(left[:64], faces[4][0][:64], faces[4][1][64:]).astype(BF)
    meta_row = lax.broadcasted_iota(jnp.int32, (16, 128), 0)
    send[320:336, :] = jnp.where(
        meta_row == 0,
        jnp.broadcast_to(route_ref[...].astype(F32), (16, 128)),
        jnp.broadcast_to(elem_ref[...].astype(F32), (16, 128)),
    ).astype(BF)

    pl.semaphore_wait(barrier, 14)
    edge_copies = []
    for n, dev in enumerate(edge_peers):
        rows = pl.ds(8 * n, 8)
        copy = pltpu.make_async_remote_copy(
            src_ref=edge_send.at[rows],
            dst_ref=edge_got.at[rows],
            send_sem=edge_send_sem.at[n],
            recv_sem=edge_recv_sem.at[n],
            device_id=dev,
            device_id_type=mesh_id,
        )
        copy.start()
        edge_copies.append(copy)
    copies = []
    for n, dev in enumerate(peers):
        copy = pltpu.make_async_remote_copy(
            src_ref=send,
            dst_ref=got.at[n],
            send_sem=send_sem.at[n],
            recv_sem=recv_sem.at[n],
            device_id=dev,
            device_id_type=mesh_id,
        )
        copy.start()
        copies.append(copy)

    for f in range(5):
        x[f, :, 128:256] = x[f, :, 128:256] * keep
        x[f, :, 256:384] = x[f, :, 256:384] * keep
        low_pad[f, 8:136, :] = x[f, :, 0:128] * keep
        high_pad[f, 8:136, :] = x[f, :, 384:512] * keep
        above = low_pad[f, 9:137, :]
        below = high_pad[f, 7:135, :]
        x[f, :, 0:128] = low_pad[f, 8:136, :] + jnp.where(left, pltpu.roll(below, 64, 1), 0.0)
        x[f, :, 384:512] = high_pad[f, 8:136, :] + jnp.where(left, 0.0, pltpu.roll(above, 64, 1))
    for copy in later_loads:
        copy.wait()
    apply_operator(x, met, vel, i_tab, jk_tab, out_ref)

    wide = lax.broadcasted_iota(jnp.int32, (128, 512), 1)
    on_low = lax.rem(wide, 64) < 8
    weight = met[1] * viscosity * vecs[0:1, :] + jnp.where(on_low, vel[1], 0.0)
    wh, wl = halves_of(weight)
    for cols in HALF:
        w_ref[:, cols] = (
            mmt(wh[:, cols], jk_tab[0, 0])
            + mmt(wl[:, cols], jk_tab[0, 0])
            + mmt(wh[:, cols], jk_tab[0, 1])
        )

    def low_nodes(src):
        ah, al = halves_of(src[0])
        bh, bl = halves_of(src[2])
        return (
            mm(ah, pick[:, 0:128])
            + mm(al, pick[:, 0:128])
            + mm(bh, pick[:, 128:256])
            + mm(bl, pick[:, 128:256])
        )

    face_met[...] = low_nodes(met) * viscosity
    face_vel[...] = low_nodes(vel)

    edge_rows = lax.broadcasted_iota(jnp.int32, (16, 512), 0)
    edge_wide = lax.broadcasted_iota(jnp.int32, (16, 512), 1)
    head = edge_rows < 8

    def ends(src, dim):
        a = jnp.broadcast_to(src[dim, 0:1, :], (16, 512))
        b = jnp.broadcast_to(src[dim, 127:128, :], (16, 512))
        return a, b

    ma, mb = ends(met, 0)
    va, vb = ends(vel, 0)
    ea = ma * viscosity * vecs[1:2, :] + jnp.where(edge_wide < 64, va, 0.0)
    eb = mb * viscosity * vecs[2:3, :] + jnp.where(edge_wide >= 448, vb, 0.0)
    eh, el = halves_of(jnp.where(head, ea, eb))
    for cols in HALF:
        acc = jnp.zeros((16, 256), F32)
        for rows in HALF:
            acc += mmt(eh[:, rows], i_tab[0, cols, rows])
            acc += mmt(el[:, rows], i_tab[0, cols, rows])
            acc += mmt(eh[:, rows], i_tab[1, cols, rows])
        wi_ref[:, cols] = acc
    left16 = left[:16]
    head16 = row[:16] < 8

    def end_faces(src):
        j0, j7 = ends(src, 1)
        k0, k7 = ends(src, 2)
        a = jnp.where(left16, j0[:, 0:128], pltpu.roll(k0[:, 0:128], 64, 1))
        b = jnp.where(left16, pltpu.roll(j7[:, 384:512], 64, 1), k7[:, 384:512])
        return jnp.where(head16, a, b)

    edge_met[...] = end_faces(met) * viscosity
    edge_vel[...] = end_faces(vel)

    def absorb(sums, block):
        route = block[320:321, :].astype(F32)
        elem = block[321:322, :].astype(F32)
        dest = jnp.where(route == dom.astype(F32), elem, -1.0)
        hit = (jnp.broadcast_to(dest, (128, 128)) == row.astype(F32)).astype(F32).astype(BF)
        tail = block[256:320, :].astype(F32)
        last = jnp.concatenate(
            [jnp.where(left[:64], tail, 0.0), jnp.where(left[:64], 0.0, tail)], axis=0
        ).astype(BF)
        return [
            sums[0] + mm(hit, block[0:128, :]),
            sums[1] + mm(hit, block[128:256, :]),
            sums[2] + mm(hit, last),
        ]

    sums = absorb([jnp.zeros((128, 128), F32)] * 3, send)
    for n, copy in enumerate(copies):
        copy.wait_recv()
        sums = absorb(sums, got.at[n])
    sums[2] = sums[2] + pltpu.roll(sums[2], 64, 1)

    node = lax.rem(lane, 64)
    for c in range(3):
        mortar_pad[c, 8:136, :] = sums[c]
    for c in range(3):
        above = mortar_pad[c, 9:137, :]
        below = mortar_pad[c, 7:135, :]
        shared = (
            sums[c]
            + jnp.where(node >= 56, pltpu.roll(above, 56, 1), 0.0)
            + jnp.where(node < 8, pltpu.roll(below, 72, 1), 0.0)
        )
        flipped = pltpu.roll(shared, 64, 1)
        pair = side_by_side(shared)
        slopes = mm(pair, late[:, FORWARD : FORWARD + 256]) + mm(
            pair, late[:, FORWARD + 256 : FORWARD + 512]
        )
        for g in range(2 if c < 2 else 1):
            f = 2 * c + g
            twice = jnp.where(left == (g == 0), shared, flipped)
            inner = face_met[...] * slopes[:, 128 * g : 128 * g + 128] + face_vel[...] * twice
            inner = side_by_side(inner)
            for n, cols in enumerate(HALF):
                at = 256 * n
                everywhere = mm(pair, late[:, EXPAND + 512 * g + at : EXPAND + 512 * g + at + 256])
                low_face = mm(inner, late[:, DOWN + at : DOWN + at + 256]) + mm(
                    inner, late[:, DOWN + 512 + at : DOWN + 512 + at + 256]
                )
                out_ref[f, :, cols] = out_ref[f, :, cols] + everywhere * w_ref[:, cols] + low_face

    for copy in edge_copies:
        copy.wait_recv()
    tiles = [edge_got[8 * n : 8 * n + 8, :] for n in range(10)]
    high_tile = tiles[0] + tiles[1] + tiles[2] + tiles[3] + tiles[4]
    low_tile = tiles[5] + tiles[6] + tiles[7] + tiles[8] + tiles[9]
    lane8 = lane[:8]
    at_high = (lane8 >= 64) & (lane8 < 72)
    at_low = lane8 < 8
    highs = [jnp.where(at_high, pltpu.roll(high_tile, n, 1), 0.0) for n in (8, 72)]
    lows = [jnp.where(at_low, low_tile, 0.0), jnp.where(at_low, pltpu.roll(low_tile, 64, 1), 0.0)]
    for f in range(5):
        c, g = divmod(f, 2)
        edge_face[0, f : f + 1, :] = high_tile[3 + f : 4 + f, :] + highs[g][c : c + 1, :]
        edge_face[1, f : f + 1, :] = low_tile[3 + f : 4 + f, :] + lows[g][c : c + 1, :]
    has_next = jnp.where(place < total - 1, 1.0, 0.0)
    has_prev = jnp.where(place > 0, 1.0, 0.0)
    from_prev = edge_face[0] * has_prev
    from_next = edge_face[1] * has_next
    face = jnp.concatenate(
        [
            jnp.where(left[:8], pltpu.roll(from_prev, 64, 1), from_prev),
            jnp.where(left[:8], from_next, pltpu.roll(from_next, 64, 1)),
        ],
        axis=0,
    )
    slope = mm(side_by_side(face), late[:, SINGLE : SINGLE + 128])
    inner = side_by_side(edge_met[...] * slope + edge_vel[...] * face)
    back = mm(inner, late[:, SINGLE_BACK : SINGLE_BACK + 128]) + mm(
        inner, late[:, SINGLE_BACK + 128 : SINGLE_BACK + 256]
    )
    part = jnp.concatenate([face] * 4, axis=1) * wi_ref[...]
    part = part + jnp.concatenate(
        [
            jnp.where(head16 & left16, back, 0.0),
            jnp.zeros((16, 256), F32),
            jnp.where(head16 | left16, 0.0, back),
        ],
        axis=1,
    )
    for f in range(5):
        out_ref[f, 0:1, :] = out_ref[f, 0:1, :] + part[f : f + 1, :]
        out_ref[f, 127:128, :] = out_ref[f, 127:128, :] + part[8 + f : 9 + f, :]

    for copy in copies:
        copy.wait_send()
    for copy in edge_copies:
        copy.wait_send()


def shards(n_dom, n_sub, adjoint_field, metric, velocity, route, element, code, hanging):
    fields = [jnp.transpose(a, (1, 0, 2)) for a in (adjoint_field, metric, velocity)]
    rows = [a.reshape(1, 128) for a in (route, element, code, hanging)]
    consts = [jnp.asarray(t) for t in tables()]
    operands = [pltpu.with_memory_space_constraint(a, pltpu.HBM) for a in fields + rows + consts]
    result = pl.pallas_call(
        functools.partial(kernel, n_dom, n_sub),
        out_shape=pltpu.VMEM((5, 128, 512), F32),
        in_specs=[pl.BlockSpec(memory_space=pltpu.HBM)] * len(operands),
        out_specs=pl.BlockSpec(memory_space=pltpu.VMEM),
        scratch_shapes=[pltpu.VMEM(a.shape, a.dtype) for a in operands]
        + [
            pltpu.VMEM((ROWS, 128), BF),
            pltpu.VMEM((4, ROWS, 128), BF),
            pltpu.VMEM((80, 128), F32),
            pltpu.VMEM((80, 128), F32),
            pltpu.VMEM((2, 8, 128), F32),
            pltpu.VMEM((5, 144, 128), F32),
            pltpu.VMEM((5, 144, 128), F32),
            pltpu.VMEM((3, 144, 128), F32),
            pltpu.VMEM((128, 512), F32),
            pltpu.VMEM((128, 128), F32),
            pltpu.VMEM((128, 128), F32),
            pltpu.VMEM((16, 512), F32),
            pltpu.VMEM((16, 128), F32),
            pltpu.VMEM((16, 128), F32),
            pltpu.SemaphoreType.DMA((17,)),
            pltpu.SemaphoreType.DMA((4,)),
            pltpu.SemaphoreType.DMA((4,)),
            pltpu.SemaphoreType.DMA((10,)),
            pltpu.SemaphoreType.DMA((10,)),
        ],
        compiler_params=pltpu.CompilerParams(
            collective_id=0, has_side_effects=True, vmem_limit_bytes=40 << 20
        ),
        name="adjoint",
    )(*operands)
    return jnp.transpose(result, (1, 0, 2))


def solution(mesh):
    sizes = dict(zip(mesh.axis_names, mesh.devices.shape))
    block = P(("dom", "sub"), None, None)
    flat = P(("dom", "sub"), None)
    return jax.shard_map(
        functools.partial(shards, sizes["dom"], sizes["sub"]),
        mesh=mesh,
        in_specs=(block, block, block, flat, flat, flat, flat),
        out_specs=block,
        check_vma=False,
    )
```

```python
import functools

import jax
import jax.numpy as jnp
import ml_dtypes
import numpy as np
from jax import lax
from jax.experimental import pallas as pl
from jax.experimental.pallas import tpu as pltpu
from jax.sharding import PartitionSpec as P

gll_nodes = np.array(
    [
        -1.0,
        -0.8717401485096066,
        -0.5917001814331423,
        -0.2092992179024789,
        0.2092992179024789,
        0.5917001814331423,
        0.8717401485096066,
        1.0,
    ]
)
viscosity = 0.005
OFFSETS = (-2, -1, 1, 2)
BF = jnp.bfloat16
F32 = jnp.float32


def legendre_seven(points):
    prev = np.ones(points.shape)
    curr = np.array(points)
    for order in range(1, 7):
        nxt = ((2 * order + 1) * points * curr - order * prev) / (order + 1)
        prev, curr = (curr, nxt)
    return curr


def diff_matrix():
    values = legendre_seven(gll_nodes)
    mat = np.zeros((8, 8))
    for row in range(8):
        for col in range(8):
            if row != col:
                mat[row, col] = values[row] / (values[col] * (gll_nodes[row] - gll_nodes[col]))
    mat[0, 0] = -14.0
    mat[7, 7] = 14.0
    return mat


def lagrange_at(points):
    basis = np.ones((8, 8))
    for row in range(8):
        for col in range(8):
            for other in range(8):
                if other != col:
                    basis[row, col] *= (points[row] - gll_nodes[other]) / (
                        gll_nodes[col] - gll_nodes[other]
                    )
    return basis


def split(mat):
    mat = np.asarray(mat, np.float32)
    high = mat.astype(ml_dtypes.bfloat16)
    low = (mat - high.astype(np.float32)).astype(ml_dtypes.bfloat16)
    return np.stack([high, low])


def fold_table():
    parts = [lagrange_at((gll_nodes - 1.0) / 2.0), lagrange_at((gll_nodes + 1.0) / 2.0)]
    turn = np.zeros((64, 64))
    for col in range(64):
        turn[col % 8 * 8 + col // 8, col] = 1.0
    mats = []
    for code in range(8):
        mat = np.kron(parts[code % 2], parts[code // 2 % 2])
        mats.append(mat @ turn if code >= 4 else mat)
    high, low = split(np.stack(mats, axis=1))
    table = np.zeros((2, 2, 8, 8, 8, 64), np.float32)
    for i in range(8):
        a, b = divmod(i, 2)
        rows = slice(8 * i, 8 * i + 8)
        table[0, b, 7 - a] = high[rows].astype(np.float32)
        table[0, b, 3 - a] = high[rows].astype(np.float32)
        table[1, b, 7 - a] = low[rows].astype(np.float32)
    return table.reshape(256, 512).astype(ml_dtypes.bfloat16)


def face_derivatives(dmat):
    eye = np.eye(8)
    return np.kron(dmat, eye).T, np.kron(eye, dmat).T


def to_low_face():
    table = np.zeros((8, 8, 8, 8, 8))
    for i in range(8):
        for k in range(8):
            table[i, k, i, 0, k] = 1.0
    return table.reshape(64, 512)


def tables():
    dmat = diff_matrix().astype(np.float32)
    eye = np.eye(8)
    along_i = np.kron(np.kron(dmat, eye), eye).T
    along_j = np.kron(np.kron(np.eye(4), dmat), eye).T
    along_k = np.kron(np.kron(np.eye(4), eye), dmat).T
    i_tab = split(along_i)
    jk_tab = np.stack([split(along_j), split(along_k)])

    first, second = face_derivatives(dmat)
    both = np.concatenate([first, second], axis=1)
    zero = np.zeros((64, 128))
    high, low = [t.astype(np.float32) for t in split(both)]
    pair_high = np.block([[high, zero], [zero, high]])
    pair_low = np.block([[low, zero], [zero, low]])
    forward = np.stack(
        [np.concatenate([pair_high, pair_high]), np.concatenate([pair_low, 0 * pair_low])]
    )
    single = np.concatenate([high, low, high, 0 * high])
    back = both.T
    spread = to_low_face()
    bh, bl = [t.astype(np.float32) for t in split(back)]
    down = np.stack(
        [np.concatenate([bh, bh]) @ spread, np.concatenate([bl, 0 * bl]) @ spread]
    )
    twice = np.concatenate([np.eye(64), np.eye(64)], axis=1)
    single_back = np.stack(
        [np.concatenate([bh, bh]) @ twice, np.concatenate([bl, 0 * bl]) @ twice]
    )
    every = np.zeros((8, 8, 8, 8, 8))
    for i in range(8):
        for k in range(8):
            every[i, k, i, :, k] = 1.0
    every = every.reshape(64, 512)
    none = np.zeros((64, 512))
    expand = np.stack(
        [
            np.concatenate([every, none, every, none]),
            np.concatenate([none, every, none, every]),
        ]
    )
    gather = spread.T
    blank = np.zeros((512, 64))
    pick = np.concatenate([gather, blank, blank, gather], axis=1)
    cast = lambda t: np.asarray(t, np.float32).astype(ml_dtypes.bfloat16)
    vecs = np.zeros((8, 8, 8, 8), np.float32)
    vecs[0] = dmat[:, 0][None, :, None]
    vecs[1] = dmat[:, 0][:, None, None]
    vecs[2] = dmat[:, 7][:, None, None]
    late = np.concatenate(
        [expand[0], expand[1], down[0], down[1], forward[0], forward[1], single]
        + [single_back[0], single_back[1], np.zeros((256, 128))],
        axis=1,
    )
    return (
        fold_table(),
        i_tab,
        jk_tab,
        cast(pick),
        cast(late),
        vecs.reshape(8, 512),
    )


def halves_of(value):
    high = value.astype(BF)
    low = (value - high.astype(F32)).astype(BF)
    return high, low


def mm(a, b):
    return jnp.dot(a, b, preferred_element_type=F32)


def mmt(a, b):
    return lax.dot_general(a, b, (((1,), (1,)), ((), ())), preferred_element_type=F32)


def side_by_side(value):
    return jnp.concatenate(halves_of(value), axis=1)


ROWS = 336
HALF = [slice(0, 256), slice(256, 512)]
EXPAND, DOWN, FORWARD, SINGLE, SINGLE_BACK = 0, 1024, 2048, 2560, 2688


def apply_operator(x, met, vel, i_tab, jk_tab, out_ref):
    high, low = halves_of(x[...].reshape(640, 512))

    def inner(dim, cols, derived):
        m = met[dim, :, cols] * viscosity
        v = vel[dim, :, cols]
        value = derived.reshape(5, 128, 256) * m[None] + x[:, :, cols] * v[None]
        return halves_of(value.reshape(640, 256))

    parts_i = []
    for cols in HALF:
        derived = jnp.zeros((640, 256), F32)
        for rows in HALF:
            derived += mm(high[:, rows], i_tab[0, rows, cols])
            derived += mm(low[:, rows], i_tab[0, rows, cols])
            derived += mm(high[:, rows], i_tab[1, rows, cols])
        parts_i.append(inner(0, cols, derived))
    for cols in HALF:
        total = jnp.zeros((640, 256), F32)
        for m, rows in enumerate(HALF):
            a, b = parts_i[m]
            total += mmt(a, i_tab[0, cols, rows])
            total += mmt(b, i_tab[0, cols, rows])
            total += mmt(a, i_tab[1, cols, rows])
        for dim in (1, 2):
            derived = mm(high[:, cols], jk_tab[dim - 1, 0])
            derived += mm(low[:, cols], jk_tab[dim - 1, 0])
            derived += mm(high[:, cols], jk_tab[dim - 1, 1])
            a, b = inner(dim, cols, derived)
            total += mmt(a, jk_tab[dim - 1, 0])
            total += mmt(b, jk_tab[dim - 1, 0])
            total += mmt(a, jk_tab[dim - 1, 1])
        out_ref[:, :, cols] = total.reshape(5, 128, 256)


def kernel(n_dom, n_sub, *refs):
    (x_hbm, met_hbm, vel_hbm, route_hbm, elem_hbm, code_hbm, hang_hbm) = refs[:7]
    (fold_hbm, i_hbm, jk_hbm, pick_hbm, late_hbm, vecs_hbm) = refs[7:13]
    (out_ref, shared_ref, ends_ref, w_ref, face_met, face_vel, late) = refs[13:20]
    (x, met, vel, route_ref, elem_ref, code_ref, hang_ref) = refs[20:27]
    (fold, i_tab, jk_tab, pick, vecs) = refs[27:32]
    (send, got, edge_send, edge_got, edge_face, low_pad, high_pad, mortar_pad) = refs[32:40]
    (wi_ref, edge_met, edge_vel) = refs[40:43]
    (load_sem, send_sem, recv_sem, edge_send_sem, edge_recv_sem) = refs[43:48]

    dom = lax.axis_index("dom")
    sub = lax.axis_index("sub")
    mesh_id = pl.DeviceIdType.MESH
    place = dom * n_sub + sub
    total = n_dom * n_sub

    def along(offset):
        at = dom + offset
        at = jnp.where(at < 0, at + n_dom, at)
        return jnp.where(at >= n_dom, at - n_dom, at)

    peers = [{"dom": along(o), "sub": sub} for o in OFFSETS]
    last, first = sub == n_sub - 1, sub == 0
    sub_up = jnp.where(last, 0, sub + 1)
    sub_down = jnp.where(first, n_sub - 1, sub - 1)
    dom_up = jnp.where(last, 1, 0)
    dom_down = jnp.where(first, -1, 0)
    edge_peers = [{"dom": along(o + dom_up), "sub": sub_up} for o in range(-2, 3)]
    edge_peers += [{"dom": along(o + dom_down), "sub": sub_down} for o in range(-2, 3)]

    loads = []

    def load(src, dst):
        copy = pltpu.make_async_copy(src, dst, load_sem.at[len(loads)])
        copy.start()
        loads.append(copy)
        return copy

    x_loads = [load(x_hbm.at[f], x.at[f]) for f in range(5)]
    first_loads = [
        load(code_hbm, code_ref),
        load(hang_hbm, hang_ref),
        load(route_hbm, route_ref),
        load(elem_hbm, elem_ref),
        load(fold_hbm, fold),
    ]
    barrier = pltpu.get_barrier_semaphore()
    for dev in peers + edge_peers:
        pl.semaphore_signal(barrier, inc=1, device_id=dev, device_id_type=mesh_id)

    lane = lax.broadcasted_iota(jnp.int32, (128, 128), 1)
    row = lax.broadcasted_iota(jnp.int32, (128, 128), 0)
    left = lane < 64
    slot = lax.rem(lane, 64) // 8

    for f in range(5):
        low_pad[f, 136:144, :] = jnp.zeros((8, 128), F32)
        high_pad[f, 0:8, :] = jnp.zeros((8, 128), F32)
    edge_face[...] = jnp.zeros((2, 8, 128), F32)
    for c in range(3):
        mortar_pad[c, 0:8, :] = jnp.zeros((8, 128), F32)
        mortar_pad[c, 136:144, :] = jnp.zeros((8, 128), F32)

    for copy in first_loads:
        copy.wait()

    def column(ref):
        return jnp.broadcast_to(ref[...].astype(F32), (128, 128)).T

    code = column(code_ref).astype(jnp.int32)
    hang = column(hang_ref)
    odd = lax.rem(code, 2) == 1

    keep = jnp.where(slot == 7, 1.0 - hang, 1.0)
    for copy in x_loads:
        copy.wait()
    later_loads = [
        load(i_hbm, i_tab),
        load(jk_hbm, jk_tab),
        load(met_hbm, met),
        load(vel_hbm, vel),
        load(pick_hbm, pick),
        load(late_hbm, late),
        load(vecs_hbm, vecs),
    ]
    lefts = []
    for f in range(5):
        packed = jnp.where(
            slot == 7,
            x[f, :, 0:128],
            jnp.where(
                slot == 6,
                pltpu.roll(x[f, :, 128:256], 120, 1),
                jnp.where(
                    slot == 5,
                    pltpu.roll(x[f, :, 256:384], 112, 1),
                    pltpu.roll(x[f, :, 384:512], 104, 1),
                ),
            ),
        )
        high = packed.astype(BF)
        low = packed - high.astype(F32)
        mixed = jnp.where(slot >= 4, packed, pltpu.roll(low, 96, 1)).astype(BF)
        lefts.append(jnp.concatenate([mixed, high], axis=1))
    mapped = mm(jnp.concatenate(lefts, axis=0), fold[...])
    faces = []
    for f in range(5):
        one = mapped[128 * f : 128 * f + 128]
        picked = jnp.where(
            code < 4,
            jnp.where(code < 2, one[:, 0:128], one[:, 128:256]),
            jnp.where(code < 6, one[:, 256:384], one[:, 384:512]),
        )
        picked = picked * hang
        other = pltpu.roll(picked, 64, 1)
        faces.append((jnp.where(odd, other, picked), jnp.where(odd, picked, other)))
    pairs = [
        jnp.where(left, faces[0][0], faces[1][1]).astype(BF),
        jnp.where(left, faces[2][0], faces[3][1]).astype(BF),
        faces[4][0].astype(BF),
    ]
    edge_row = lax.broadcasted_iota(jnp.int32, (80, 128), 0)
    tile = edge_row // 8
    part = lax.rem(edge_row, 8)
    wanted_elem = jnp.where(tile < 5, 127, 0)
    wanted_dom = lax.rem(dom + lax.rem(tile, 5) - 2 + n_dom, n_dom)
    chosen = (jnp.broadcast_to(route_ref[...], (80, 128)) == wanted_dom) & (
        jnp.broadcast_to(elem_ref[...], (80, 128)) == wanted_elem
    )
    chosen = jnp.where(chosen, 1.0, 0.0)
    edge_sums = jnp.zeros((80, 128), F32)
    for c in range(3):
        edge_sums += mm(jnp.where(part == c, chosen, 0.0).astype(BF), pairs[c])
    edge_send[...] = edge_sums
    for f in range(5):
        edge_send[19 + f : 20 + f, :] = x[f, 127:128, 384:512] * keep[127:128, :]
        edge_send[59 + f : 60 + f, :] = x[f, 0:1, 0:128] * keep[0:1, :]
    send[0:128, :] = pairs[0]
    send[128:256, :] = pairs[1]
    send[256:320, :] = jnp.where(left[:64], faces[4][0][:64], faces[4][1][64:]).astype(BF)
    meta_row = lax.broadcasted_iota(jnp.int32, (16, 128), 0)
    send[320:336, :] = jnp.where(
        meta_row == 0,
        jnp.broadcast_to(route_ref[...].astype(F32), (16, 128)),
        jnp.broadcast_to(elem_ref[...].astype(F32), (16, 128)),
    ).astype(BF)

    pl.semaphore_wait(barrier, 14)
    edge_copies, copies = [None] * 10, [None] * 4

    def send_edge(n):
        rows = pl.ds(8 * n, 8)
        edge_copies[n] = pltpu.make_async_remote_copy(
            src_ref=edge_send.at[rows],
            dst_ref=edge_got.at[rows],
            send_sem=edge_send_sem.at[n],
            recv_sem=edge_recv_sem.at[n],
            device_id=edge_peers[n],
            device_id_type=mesh_id,
        )
        edge_copies[n].start()

    def send_faces(n):
        copies[n] = pltpu.make_async_remote_copy(
            src_ref=send,
            dst_ref=got.at[n],
            send_sem=send_sem.at[n],
            recv_sem=recv_sem.at[n],
            device_id=peers[n],
            device_id_type=mesh_id,
        )
        copies[n].start()

    for n in (4, 9, 3, 8):
        send_edge(n)
    send_faces(3)
    send_faces(2)
    for n in (2, 7, 1, 6, 0, 5):
        send_edge(n)
    send_faces(1)
    send_faces(0)

    for f in range(5):
        x[f, :, 128:256] = x[f, :, 128:256] * keep
        x[f, :, 256:384] = x[f, :, 256:384] * keep
        low_pad[f, 8:136, :] = x[f, :, 0:128] * keep
        high_pad[f, 8:136, :] = x[f, :, 384:512] * keep
        above = low_pad[f, 9:137, :]
        below = high_pad[f, 7:135, :]
        x[f, :, 0:128] = low_pad[f, 8:136, :] + jnp.where(left, pltpu.roll(below, 64, 1), 0.0)
        x[f, :, 384:512] = high_pad[f, 8:136, :] + jnp.where(left, 0.0, pltpu.roll(above, 64, 1))
    for copy in later_loads:
        copy.wait()
    apply_operator(x, met, vel, i_tab, jk_tab, out_ref)

    wide = lax.broadcasted_iota(jnp.int32, (128, 512), 1)
    on_low = lax.rem(wide, 64) < 8
    weight = met[1] * viscosity * vecs[0:1, :] + jnp.where(on_low, vel[1], 0.0)
    wh, wl = halves_of(weight)
    for cols in HALF:
        w_ref[:, cols] = (
            mmt(wh[:, cols], jk_tab[0, 0])
            + mmt(wl[:, cols], jk_tab[0, 0])
            + mmt(wh[:, cols], jk_tab[0, 1])
        )

    def low_nodes(src):
        ah, al = halves_of(src[0])
        bh, bl = halves_of(src[2])
        return (
            mm(ah, pick[:, 0:128])
            + mm(al, pick[:, 0:128])
            + mm(bh, pick[:, 128:256])
            + mm(bl, pick[:, 128:256])
        )

    face_met[...] = low_nodes(met) * viscosity
    face_vel[...] = low_nodes(vel)

    edge_rows = lax.broadcasted_iota(jnp.int32, (16, 512), 0)
    edge_wide = lax.broadcasted_iota(jnp.int32, (16, 512), 1)
    head = edge_rows < 8

    def ends(src, dim):
        a = jnp.broadcast_to(src[dim, 0:1, :], (16, 512))
        b = jnp.broadcast_to(src[dim, 127:128, :], (16, 512))
        return a, b

    ma, mb = ends(met, 0)
    va, vb = ends(vel, 0)
    ea = ma * viscosity * vecs[1:2, :] + jnp.where(edge_wide < 64, va, 0.0)
    eb = mb * viscosity * vecs[2:3, :] + jnp.where(edge_wide >= 448, vb, 0.0)
    eh, el = halves_of(jnp.where(head, ea, eb))
    for cols in HALF:
        acc = jnp.zeros((16, 256), F32)
        for rows in HALF:
            acc += mmt(eh[:, rows], i_tab[0, cols, rows])
            acc += mmt(el[:, rows], i_tab[0, cols, rows])
            acc += mmt(eh[:, rows], i_tab[1, cols, rows])
        wi_ref[:, cols] = acc
    left16 = left[:16]
    head16 = row[:16] < 8

    def end_faces(src):
        j0, j7 = ends(src, 1)
        k0, k7 = ends(src, 2)
        a = jnp.where(left16, j0[:, 0:128], pltpu.roll(k0[:, 0:128], 64, 1))
        b = jnp.where(left16, pltpu.roll(j7[:, 384:512], 64, 1), k7[:, 384:512])
        return jnp.where(head16, a, b)

    edge_met[...] = end_faces(met) * viscosity
    edge_vel[...] = end_faces(vel)

    def absorb(sums, block):
        route = block[320:321, :].astype(F32)
        elem = block[321:322, :].astype(F32)
        dest = jnp.where(route == dom.astype(F32), elem, -1.0)
        hit = (jnp.broadcast_to(dest, (128, 128)) == row.astype(F32)).astype(F32).astype(BF)
        tail = block[256:320, :].astype(F32)
        last = jnp.concatenate(
            [jnp.where(left[:64], tail, 0.0), jnp.where(left[:64], 0.0, tail)], axis=0
        ).astype(BF)
        return [
            sums[0] + mm(hit, block[0:128, :]),
            sums[1] + mm(hit, block[128:256, :]),
            sums[2] + mm(hit, last),
        ]

    sums = absorb([jnp.zeros((128, 128), F32)] * 3, send)
    for n in (0, 1, 2, 3):
        copies[n].wait_recv()
        sums = absorb(sums, got.at[n])
    sums[2] = sums[2] + pltpu.roll(sums[2], 64, 1)

    node = lax.rem(lane, 64)
    for c in range(3):
        mortar_pad[c, 8:136, :] = sums[c]
    for c in range(3):
        above = mortar_pad[c, 9:137, :]
        below = mortar_pad[c, 7:135, :]
        shared_ref[c] = (
            sums[c]
            + jnp.where(node >= 56, pltpu.roll(above, 56, 1), 0.0)
            + jnp.where(node < 8, pltpu.roll(below, 72, 1), 0.0)
        )

    for copy in edge_copies:
        copy.wait_recv()
    tiles = [edge_got[8 * n : 8 * n + 8, :] for n in range(10)]
    high_tile = tiles[0] + tiles[1] + tiles[2] + tiles[3] + tiles[4]
    low_tile = tiles[5] + tiles[6] + tiles[7] + tiles[8] + tiles[9]
    lane8 = lane[:8]
    at_high = (lane8 >= 64) & (lane8 < 72)
    at_low = lane8 < 8
    highs = [jnp.where(at_high, pltpu.roll(high_tile, n, 1), 0.0) for n in (8, 72)]
    lows = [jnp.where(at_low, low_tile, 0.0), jnp.where(at_low, pltpu.roll(low_tile, 64, 1), 0.0)]
    for f in range(5):
        c, g = divmod(f, 2)
        edge_face[0, f : f + 1, :] = high_tile[3 + f : 4 + f, :] + highs[g][c : c + 1, :]
        edge_face[1, f : f + 1, :] = low_tile[3 + f : 4 + f, :] + lows[g][c : c + 1, :]
    has_next = jnp.where(place < total - 1, 1.0, 0.0)
    has_prev = jnp.where(place > 0, 1.0, 0.0)
    from_prev = edge_face[0] * has_prev
    from_next = edge_face[1] * has_next
    face = jnp.concatenate(
        [
            jnp.where(left[:8], pltpu.roll(from_prev, 64, 1), from_prev),
            jnp.where(left[:8], from_next, pltpu.roll(from_next, 64, 1)),
        ],
        axis=0,
    )
    slope = mm(side_by_side(face), late[:, SINGLE : SINGLE + 128])
    inner = side_by_side(edge_met[...] * slope + edge_vel[...] * face)
    back = mm(inner, late[:, SINGLE_BACK : SINGLE_BACK + 128]) + mm(
        inner, late[:, SINGLE_BACK + 128 : SINGLE_BACK + 256]
    )
    part = jnp.concatenate([face] * 4, axis=1) * wi_ref[...]
    part = part + jnp.concatenate(
        [
            jnp.where(head16 & left16, back, 0.0),
            jnp.zeros((16, 256), F32),
            jnp.where(head16 | left16, 0.0, back),
        ],
        axis=1,
    )
    ends_ref[...] = part

    for copy in copies:
        copy.wait_send()
    for copy in edge_copies:
        copy.wait_send()


def finish_kernel(local, shared_ref, ends_ref, w_ref, face_met, face_vel, late, out_hbm, res, sem):
    left = lax.broadcasted_iota(jnp.int32, (128, 128), 1) < 64
    shared = [shared_ref[c] for c in range(3)]
    pairs = jnp.concatenate([side_by_side(part) for part in shared], axis=0)
    slopes = mm(pairs, late[:, FORWARD : FORWARD + 256]) + mm(
        pairs, late[:, FORWARD + 256 : FORWARD + 512]
    )
    inners = []
    for f in range(5):
        c, g = divmod(f, 2)
        twice = jnp.where(left == (g == 0), shared[c], pltpu.roll(shared[c], 64, 1))
        slope = slopes[128 * c : 128 * c + 128, 128 * g : 128 * g + 128]
        inners.append(side_by_side(face_met[...] * slope + face_vel[...] * twice))
    inners = jnp.concatenate(inners, axis=0)
    every, lows = [], []
    for at in (0, 256):
        even = mm(pairs, late[:, EXPAND + at : EXPAND + at + 256])
        odd = mm(pairs[:256], late[:, EXPAND + 512 + at : EXPAND + 512 + at + 256])
        every.append((even, odd))
        lows.append(
            mm(inners, late[:, DOWN + at : DOWN + at + 256])
            + mm(inners, late[:, DOWN + 512 + at : DOWN + 512 + at + 256])
        )
    copies = []
    for f in range(5):
        c, g = divmod(f, 2)
        for n, cols in enumerate(HALF):
            spread = every[n][g][128 * c : 128 * c + 128]
            low = lows[n][128 * f : 128 * f + 128]
            res[f, :, cols] = local[f, :, cols] + spread * w_ref[:, cols] + low
        res[f, 0:1, :] = res[f, 0:1, :] + ends_ref[f : f + 1, :]
        res[f, 127:128, :] = res[f, 127:128, :] + ends_ref[8 + f : 9 + f, :]
        copy = pltpu.make_async_copy(res.at[f], out_hbm.at[f], sem.at[f])
        copy.start()
        copies.append(copy)
    for copy in copies:
        copy.wait()


def shards(n_dom, n_sub, adjoint_field, metric, velocity, route, element, code, hanging):
    fields = [jnp.transpose(a, (1, 0, 2)) for a in (adjoint_field, metric, velocity)]
    rows = [a.reshape(1, 128) for a in (route, element, code, hanging)]
    consts = [jnp.asarray(t) for t in tables()]
    operands = [pltpu.with_memory_space_constraint(a, pltpu.HBM) for a in fields + rows + consts]
    made = [
        pltpu.VMEM((5, 128, 512), F32),
        pltpu.VMEM((3, 128, 128), F32),
        pltpu.VMEM((16, 512), F32),
        pltpu.VMEM((128, 512), F32),
        pltpu.VMEM((128, 128), F32),
        pltpu.VMEM((128, 128), F32),
        pltpu.VMEM(consts[4].shape, BF),
    ]
    held = fields + rows + consts[:4] + consts[5:]
    handed = pl.pallas_call(
        functools.partial(kernel, n_dom, n_sub),
        out_shape=made,
        in_specs=[pl.BlockSpec(memory_space=pltpu.HBM)] * len(operands),
        out_specs=[pl.BlockSpec(memory_space=pltpu.VMEM)] * len(made),
        scratch_shapes=[pltpu.VMEM(a.shape, a.dtype) for a in held]
        + [
            pltpu.VMEM((ROWS, 128), BF),
            pltpu.VMEM((4, ROWS, 128), BF),
            pltpu.VMEM((80, 128), F32),
            pltpu.VMEM((80, 128), F32),
            pltpu.VMEM((2, 8, 128), F32),
            pltpu.VMEM((5, 144, 128), F32),
            pltpu.VMEM((5, 144, 128), F32),
            pltpu.VMEM((3, 144, 128), F32),
            pltpu.VMEM((16, 512), F32),
            pltpu.VMEM((16, 128), F32),
            pltpu.VMEM((16, 128), F32),
            pltpu.SemaphoreType.DMA((17,)),
            pltpu.SemaphoreType.DMA((4,)),
            pltpu.SemaphoreType.DMA((4,)),
            pltpu.SemaphoreType.DMA((10,)),
            pltpu.SemaphoreType.DMA((10,)),
        ],
        compiler_params=pltpu.CompilerParams(
            collective_id=0, has_side_effects=True, vmem_limit_bytes=40 << 20
        ),
        name="adjoint",
    )(*operands)
    handed = [pltpu.with_memory_space_constraint(a, pltpu.VMEM) for a in handed]
    result = pl.pallas_call(
        finish_kernel,
        out_shape=jax.ShapeDtypeStruct((5, 128, 512), F32),
        in_specs=[pl.BlockSpec(memory_space=pltpu.VMEM)] * len(handed),
        out_specs=pl.BlockSpec(memory_space=pltpu.HBM),
        scratch_shapes=[pltpu.VMEM((5, 128, 512), F32), pltpu.SemaphoreType.DMA((5,))],
        compiler_params=pltpu.CompilerParams(vmem_limit_bytes=32 << 20),
        name="finish",
    )(*handed)
    return jnp.transpose(result, (1, 0, 2))


def solution(mesh):
    sizes = dict(zip(mesh.axis_names, mesh.devices.shape))
    block = P(("dom", "sub"), None, None)
    flat = P(("dom", "sub"), None)
    return jax.shard_map(
        functools.partial(shards, sizes["dom"], sizes["sub"]),
        mesh=mesh,
        in_specs=(block, block, block, flat, flat, flat, flat),
        out_specs=block,
        check_vma=False,
    )
```

```python
import functools

import jax
import jax.numpy as jnp
import ml_dtypes
import numpy as np
from jax import lax
from jax.experimental import pallas as pl
from jax.experimental.pallas import tpu as pltpu
from jax.sharding import PartitionSpec as P

gll_nodes = np.array(
    [
        -1.0,
        -0.8717401485096066,
        -0.5917001814331423,
        -0.2092992179024789,
        0.2092992179024789,
        0.5917001814331423,
        0.8717401485096066,
        1.0,
    ]
)
viscosity = 0.005
OFFSETS = (-2, -1, 1, 2)
BF = jnp.bfloat16
F32 = jnp.float32


def legendre_seven(points):
    prev = np.ones(points.shape)
    curr = np.array(points)
    for order in range(1, 7):
        nxt = ((2 * order + 1) * points * curr - order * prev) / (order + 1)
        prev, curr = (curr, nxt)
    return curr


def diff_matrix():
    values = legendre_seven(gll_nodes)
    mat = np.zeros((8, 8))
    for row in range(8):
        for col in range(8):
            if row != col:
                mat[row, col] = values[row] / (values[col] * (gll_nodes[row] - gll_nodes[col]))
    mat[0, 0] = -14.0
    mat[7, 7] = 14.0
    return mat


def lagrange_at(points):
    basis = np.ones((8, 8))
    for row in range(8):
        for col in range(8):
            for other in range(8):
                if other != col:
                    basis[row, col] *= (points[row] - gll_nodes[other]) / (
                        gll_nodes[col] - gll_nodes[other]
                    )
    return basis


def split(mat):
    mat = np.asarray(mat, np.float32)
    high = mat.astype(ml_dtypes.bfloat16)
    low = (mat - high.astype(np.float32)).astype(ml_dtypes.bfloat16)
    return np.stack([high, low])


def fold_table():
    parts = [lagrange_at((gll_nodes - 1.0) / 2.0), lagrange_at((gll_nodes + 1.0) / 2.0)]
    turn = np.zeros((64, 64))
    for col in range(64):
        turn[col % 8 * 8 + col // 8, col] = 1.0
    mats = []
    for code in range(8):
        mat = np.kron(parts[code % 2], parts[code // 2 % 2])
        mats.append(mat @ turn if code >= 4 else mat)
    high, low = split(np.stack(mats, axis=1))
    table = np.zeros((2, 2, 8, 8, 8, 64), np.float32)
    for i in range(8):
        a, b = divmod(i, 2)
        rows = slice(8 * i, 8 * i + 8)
        table[0, b, 7 - a] = high[rows].astype(np.float32)
        table[0, b, 3 - a] = high[rows].astype(np.float32)
        table[1, b, 7 - a] = low[rows].astype(np.float32)
    return table.reshape(256, 512).astype(ml_dtypes.bfloat16)


def face_derivatives(dmat):
    eye = np.eye(8)
    return np.kron(dmat, eye).T, np.kron(eye, dmat).T


def to_low_face():
    table = np.zeros((8, 8, 8, 8, 8))
    for i in range(8):
        for k in range(8):
            table[i, k, i, 0, k] = 1.0
    return table.reshape(64, 512)


def tables():
    dmat = diff_matrix().astype(np.float32)
    eye = np.eye(8)
    along_i = np.kron(np.kron(dmat, eye), eye).T
    along_j = np.kron(np.kron(np.eye(4), dmat), eye).T
    along_k = np.kron(np.kron(np.eye(4), eye), dmat).T
    i_tab = split(along_i)
    jk_tab = np.stack([split(along_j), split(along_k)])

    first, second = face_derivatives(dmat)
    both = np.concatenate([first, second], axis=1)
    zero = np.zeros((64, 128))
    high, low = [t.astype(np.float32) for t in split(both)]
    pair_high = np.block([[high, zero], [zero, high]])
    pair_low = np.block([[low, zero], [zero, low]])
    forward = np.stack(
        [np.concatenate([pair_high, pair_high]), np.concatenate([pair_low, 0 * pair_low])]
    )
    single = np.concatenate([high, low, high, 0 * high])
    back = both.T
    spread = to_low_face()
    bh, bl = [t.astype(np.float32) for t in split(back)]
    down = np.stack(
        [np.concatenate([bh, bh]) @ spread, np.concatenate([bl, 0 * bl]) @ spread]
    )
    twice = np.concatenate([np.eye(64), np.eye(64)], axis=1)
    single_back = np.stack(
        [np.concatenate([bh, bh]) @ twice, np.concatenate([bl, 0 * bl]) @ twice]
    )
    every = np.zeros((8, 8, 8, 8, 8))
    for i in range(8):
        for k in range(8):
            every[i, k, i, :, k] = 1.0
    every = every.reshape(64, 512)
    none = np.zeros((64, 512))
    expand = np.stack(
        [
            np.concatenate([every, none, every, none]),
            np.concatenate([none, every, none, every]),
        ]
    )
    gather = spread.T
    blank = np.zeros((512, 64))
    pick = np.concatenate([gather, blank, blank, gather], axis=1)
    cast = lambda t: np.asarray(t, np.float32).astype(ml_dtypes.bfloat16)
    vecs = np.zeros((8, 8, 8, 8), np.float32)
    vecs[0] = dmat[:, 0][None, :, None]
    vecs[1] = dmat[:, 0][:, None, None]
    vecs[2] = dmat[:, 7][:, None, None]
    late = np.concatenate(
        [expand[0], expand[1], down[0], down[1], forward[0], forward[1], single]
        + [single_back[0], single_back[1], np.zeros((256, 128))],
        axis=1,
    )
    return (
        fold_table(),
        i_tab,
        jk_tab,
        cast(pick),
        cast(late),
        vecs.reshape(8, 512),
    )


def halves_of(value):
    high = value.astype(BF)
    low = (value - high.astype(F32)).astype(BF)
    return high, low


def mm(a, b):
    return jnp.dot(a, b, preferred_element_type=F32)


def mmt(a, b):
    return lax.dot_general(a, b, (((1,), (1,)), ((), ())), preferred_element_type=F32)


def side_by_side(value):
    return jnp.concatenate(halves_of(value), axis=1)


ROWS = 336
HALF = [slice(0, 256), slice(256, 512)]
EXPAND, DOWN, FORWARD, SINGLE, SINGLE_BACK = 0, 1024, 2048, 2560, 2688


def apply_operator(x, met, vel, i_tab, jk_tab, out_ref):
    high, low = halves_of(x[...].reshape(640, 512))

    def inner(dim, cols, derived):
        m = met[dim, :, cols] * viscosity
        v = vel[dim, :, cols]
        value = derived.reshape(5, 128, 256) * m[None] + x[:, :, cols] * v[None]
        return halves_of(value.reshape(640, 256))

    parts_i = []
    for cols in HALF:
        derived = jnp.zeros((640, 256), F32)
        for rows in HALF:
            derived += mm(high[:, rows], i_tab[0, rows, cols])
            derived += mm(low[:, rows], i_tab[0, rows, cols])
            derived += mm(high[:, rows], i_tab[1, rows, cols])
        parts_i.append(inner(0, cols, derived))
    for cols in HALF:
        total = jnp.zeros((640, 256), F32)
        for m, rows in enumerate(HALF):
            a, b = parts_i[m]
            total += mmt(a, i_tab[0, cols, rows])
            total += mmt(b, i_tab[0, cols, rows])
            total += mmt(a, i_tab[1, cols, rows])
        for dim in (1, 2):
            derived = mm(high[:, cols], jk_tab[dim - 1, 0])
            derived += mm(low[:, cols], jk_tab[dim - 1, 0])
            derived += mm(high[:, cols], jk_tab[dim - 1, 1])
            a, b = inner(dim, cols, derived)
            total += mmt(a, jk_tab[dim - 1, 0])
            total += mmt(b, jk_tab[dim - 1, 0])
            total += mmt(a, jk_tab[dim - 1, 1])
        out_ref[:, :, cols] = total.reshape(5, 128, 256)


def kernel(n_dom, n_sub, *refs):
    (x_hbm, met_hbm, vel_hbm, route_hbm, elem_hbm, code_hbm, hang_hbm) = refs[:7]
    (fold_hbm, i_hbm, jk_hbm, pick_hbm, late_hbm, vecs_hbm) = refs[7:13]
    (out_ref, shared_ref, ends_ref, w_ref, face_met, face_vel, late) = refs[13:20]
    (x, met, vel, route_ref, elem_ref, code_ref, hang_ref) = refs[20:27]
    (fold, i_tab, jk_tab, pick, vecs) = refs[27:32]
    (send, got, edge_send, edge_got, edge_face, low_pad, high_pad, mortar_pad) = refs[32:40]
    (wi_ref, edge_met, edge_vel) = refs[40:43]
    (load_sem, send_sem, recv_sem, edge_send_sem, edge_recv_sem) = refs[43:48]

    dom = lax.axis_index("dom")
    sub = lax.axis_index("sub")
    mesh_id = pl.DeviceIdType.MESH
    place = dom * n_sub + sub
    total = n_dom * n_sub

    def along(offset):
        at = dom + offset
        at = jnp.where(at < 0, at + n_dom, at)
        return jnp.where(at >= n_dom, at - n_dom, at)

    peers = [{"dom": along(o), "sub": sub} for o in OFFSETS]
    last, first = sub == n_sub - 1, sub == 0
    sub_up = jnp.where(last, 0, sub + 1)
    sub_down = jnp.where(first, n_sub - 1, sub - 1)
    dom_up = jnp.where(last, 1, 0)
    dom_down = jnp.where(first, -1, 0)
    edge_peers = [{"dom": along(o + dom_up), "sub": sub_up} for o in range(-2, 3)]
    edge_peers += [{"dom": along(o + dom_down), "sub": sub_down} for o in range(-2, 3)]

    loads = []

    def load(src, dst):
        copy = pltpu.make_async_copy(src, dst, load_sem.at[len(loads)])
        copy.start()
        loads.append(copy)
        return copy

    x_loads = [load(x_hbm.at[f], x.at[f]) for f in range(5)]
    first_loads = [
        load(code_hbm, code_ref),
        load(hang_hbm, hang_ref),
        load(route_hbm, route_ref),
        load(elem_hbm, elem_ref),
        load(fold_hbm, fold),
    ]
    barrier = pltpu.get_barrier_semaphore()
    for dev in peers + edge_peers:
        pl.semaphore_signal(barrier, inc=1, device_id=dev, device_id_type=mesh_id)

    lane = lax.broadcasted_iota(jnp.int32, (128, 128), 1)
    row = lax.broadcasted_iota(jnp.int32, (128, 128), 0)
    left = lane < 64
    slot = lax.rem(lane, 64) // 8

    for f in range(5):
        low_pad[f, 136:144, :] = jnp.zeros((8, 128), F32)
        high_pad[f, 0:8, :] = jnp.zeros((8, 128), F32)
    edge_face[...] = jnp.zeros((2, 8, 128), F32)
    for c in range(3):
        mortar_pad[c, 0:8, :] = jnp.zeros((8, 128), F32)
        mortar_pad[c, 136:144, :] = jnp.zeros((8, 128), F32)

    for copy in first_loads:
        copy.wait()

    def column(ref):
        return jnp.broadcast_to(ref[...].astype(F32), (128, 128)).T

    code = column(code_ref).astype(jnp.int32)
    hang = column(hang_ref)
    odd = lax.rem(code, 2) == 1

    keep = jnp.where(slot == 7, 1.0 - hang, 1.0)
    for copy in x_loads:
        copy.wait()
    later_loads = [
        load(i_hbm, i_tab),
        load(jk_hbm, jk_tab),
        load(met_hbm, met),
        load(vel_hbm, vel),
        load(pick_hbm, pick),
        load(late_hbm, late),
        load(vecs_hbm, vecs),
    ]
    lefts = []
    for f in range(5):
        packed = jnp.where(
            slot == 7,
            x[f, :, 0:128],
            jnp.where(
                slot == 6,
                pltpu.roll(x[f, :, 128:256], 120, 1),
                jnp.where(
                    slot == 5,
                    pltpu.roll(x[f, :, 256:384], 112, 1),
                    pltpu.roll(x[f, :, 384:512], 104, 1),
                ),
            ),
        )
        high = packed.astype(BF)
        low = packed - high.astype(F32)
        mixed = jnp.where(slot >= 4, packed, pltpu.roll(low, 96, 1)).astype(BF)
        lefts.append(jnp.concatenate([mixed, high], axis=1))
    mapped = mm(jnp.concatenate(lefts, axis=0), fold[...])
    faces = []
    for f in range(5):
        one = mapped[128 * f : 128 * f + 128]
        picked = jnp.where(
            code < 4,
            jnp.where(code < 2, one[:, 0:128], one[:, 128:256]),
            jnp.where(code < 6, one[:, 256:384], one[:, 384:512]),
        )
        picked = picked * hang
        other = pltpu.roll(picked, 64, 1)
        faces.append((jnp.where(odd, other, picked), jnp.where(odd, picked, other)))
    pairs = [
        jnp.where(left, faces[0][0], faces[1][1]).astype(BF),
        jnp.where(left, faces[2][0], faces[3][1]).astype(BF),
        faces[4][0].astype(BF),
    ]
    edge_row = lax.broadcasted_iota(jnp.int32, (80, 128), 0)
    tile = edge_row // 8
    part = lax.rem(edge_row, 8)
    wanted_elem = jnp.where(tile < 5, 127, 0)
    wanted_dom = lax.rem(dom + lax.rem(tile, 5) - 2 + n_dom, n_dom)
    chosen = (jnp.broadcast_to(route_ref[...], (80, 128)) == wanted_dom) & (
        jnp.broadcast_to(elem_ref[...], (80, 128)) == wanted_elem
    )
    chosen = jnp.where(chosen, 1.0, 0.0)
    edge_sums = jnp.zeros((80, 128), F32)
    for c in range(3):
        edge_sums += mm(jnp.where(part == c, chosen, 0.0).astype(BF), pairs[c])
    edge_send[...] = edge_sums
    for f in range(5):
        edge_send[19 + f : 20 + f, :] = x[f, 127:128, 384:512] * keep[127:128, :]
        edge_send[59 + f : 60 + f, :] = x[f, 0:1, 0:128] * keep[0:1, :]
    send[0:128, :] = pairs[0]
    send[128:256, :] = pairs[1]
    send[256:320, :] = jnp.where(left[:64], faces[4][0][:64], faces[4][1][64:]).astype(BF)
    meta_row = lax.broadcasted_iota(jnp.int32, (16, 128), 0)
    send[320:336, :] = jnp.where(
        meta_row == 0,
        jnp.broadcast_to(route_ref[...].astype(F32), (16, 128)),
        jnp.broadcast_to(elem_ref[...].astype(F32), (16, 128)),
    ).astype(BF)

    def edge_copy(n):
        rows = pl.ds(8 * n, 8)
        return pltpu.make_async_remote_copy(
            src_ref=edge_send.at[rows],
            dst_ref=edge_got.at[rows],
            send_sem=edge_send_sem.at[n],
            recv_sem=edge_recv_sem.at[n],
            device_id=edge_peers[n],
            device_id_type=mesh_id,
        )

    def face_copy(n):
        return pltpu.make_async_remote_copy(
            src_ref=send,
            dst_ref=got.at[n],
            send_sem=send_sem.at[n],
            recv_sem=recv_sem.at[n],
            device_id=peers[n],
            device_id_type=mesh_id,
        )

    def exchange():
        pl.semaphore_wait(barrier, 14)
        for n in (4, 9, 3, 8):
            edge_copy(n).start()
        for n in (3, 2):
            face_copy(n).start()
        for n in (2, 7, 1, 6, 0, 5):
            edge_copy(n).start()
        for n in (1, 0):
            face_copy(n).start()

    left16 = left[:16]
    head16 = row[:16] < 8

    def alone():
        for f in range(5):
            x[f, :, 128:256] = x[f, :, 128:256] * keep
            x[f, :, 256:384] = x[f, :, 256:384] * keep
            low_pad[f, 8:136, :] = x[f, :, 0:128] * keep
            high_pad[f, 8:136, :] = x[f, :, 384:512] * keep
            above = low_pad[f, 9:137, :]
            below = high_pad[f, 7:135, :]
            x[f, :, 0:128] = low_pad[f, 8:136, :] + jnp.where(left, pltpu.roll(below, 64, 1), 0.0)
            x[f, :, 384:512] = high_pad[f, 8:136, :] + jnp.where(left, 0.0, pltpu.roll(above, 64, 1))
        for copy in later_loads:
            copy.wait()
        apply_operator(x, met, vel, i_tab, jk_tab, out_ref)

        wide = lax.broadcasted_iota(jnp.int32, (128, 512), 1)
        on_low = lax.rem(wide, 64) < 8
        weight = met[1] * viscosity * vecs[0:1, :] + jnp.where(on_low, vel[1], 0.0)
        wh, wl = halves_of(weight)
        for cols in HALF:
            w_ref[:, cols] = (
                mmt(wh[:, cols], jk_tab[0, 0])
                + mmt(wl[:, cols], jk_tab[0, 0])
                + mmt(wh[:, cols], jk_tab[0, 1])
            )

        def low_nodes(src):
            ah, al = halves_of(src[0])
            bh, bl = halves_of(src[2])
            return (
                mm(ah, pick[:, 0:128])
                + mm(al, pick[:, 0:128])
                + mm(bh, pick[:, 128:256])
                + mm(bl, pick[:, 128:256])
            )

        face_met[...] = low_nodes(met) * viscosity
        face_vel[...] = low_nodes(vel)

        edge_rows = lax.broadcasted_iota(jnp.int32, (16, 512), 0)
        edge_wide = lax.broadcasted_iota(jnp.int32, (16, 512), 1)
        head = edge_rows < 8

        def ends(src, dim):
            a = jnp.broadcast_to(src[dim, 0:1, :], (16, 512))
            b = jnp.broadcast_to(src[dim, 127:128, :], (16, 512))
            return a, b

        ma, mb = ends(met, 0)
        va, vb = ends(vel, 0)
        ea = ma * viscosity * vecs[1:2, :] + jnp.where(edge_wide < 64, va, 0.0)
        eb = mb * viscosity * vecs[2:3, :] + jnp.where(edge_wide >= 448, vb, 0.0)
        eh, el = halves_of(jnp.where(head, ea, eb))
        for cols in HALF:
            acc = jnp.zeros((16, 256), F32)
            for rows in HALF:
                acc += mmt(eh[:, rows], i_tab[0, cols, rows])
                acc += mmt(el[:, rows], i_tab[0, cols, rows])
                acc += mmt(eh[:, rows], i_tab[1, cols, rows])
            wi_ref[:, cols] = acc

        def end_faces(src):
            j0, j7 = ends(src, 1)
            k0, k7 = ends(src, 2)
            a = jnp.where(left16, j0[:, 0:128], pltpu.roll(k0[:, 0:128], 64, 1))
            b = jnp.where(left16, pltpu.roll(j7[:, 384:512], 64, 1), k7[:, 384:512])
            return jnp.where(head16, a, b)

        edge_met[...] = end_faces(met) * viscosity
        edge_vel[...] = end_faces(vel)

    column_place = lax.rem(dom, 24)
    early = (column_place < 2) | ((column_place == 2) & (sub == 0))
    turn = jnp.where(early, 0, 1)

    @pl.loop(0, 2)
    def _(step):
        pl.when(step == turn)(alone)
        pl.when(step != turn)(exchange)

    def absorb(sums, block):
        route = block[320:321, :].astype(F32)
        elem = block[321:322, :].astype(F32)
        dest = jnp.where(route == dom.astype(F32), elem, -1.0)
        hit = (jnp.broadcast_to(dest, (128, 128)) == row.astype(F32)).astype(F32).astype(BF)
        tail = block[256:320, :].astype(F32)
        last = jnp.concatenate(
            [jnp.where(left[:64], tail, 0.0), jnp.where(left[:64], 0.0, tail)], axis=0
        ).astype(BF)
        return [
            sums[0] + mm(hit, block[0:128, :]),
            sums[1] + mm(hit, block[128:256, :]),
            sums[2] + mm(hit, last),
        ]

    sums = absorb([jnp.zeros((128, 128), F32)] * 3, send)
    for n in (0, 1, 2, 3):
        face_copy(n).wait_recv()
        sums = absorb(sums, got.at[n])
    sums[2] = sums[2] + pltpu.roll(sums[2], 64, 1)

    node = lax.rem(lane, 64)
    for c in range(3):
        mortar_pad[c, 8:136, :] = sums[c]
    for c in range(3):
        above = mortar_pad[c, 9:137, :]
        below = mortar_pad[c, 7:135, :]
        shared_ref[c] = (
            sums[c]
            + jnp.where(node >= 56, pltpu.roll(above, 56, 1), 0.0)
            + jnp.where(node < 8, pltpu.roll(below, 72, 1), 0.0)
        )

    for n in range(10):
        edge_copy(n).wait_recv()
    tiles = [edge_got[8 * n : 8 * n + 8, :] for n in range(10)]
    high_tile = tiles[0] + tiles[1] + tiles[2] + tiles[3] + tiles[4]
    low_tile = tiles[5] + tiles[6] + tiles[7] + tiles[8] + tiles[9]
    lane8 = lane[:8]
    at_high = (lane8 >= 64) & (lane8 < 72)
    at_low = lane8 < 8
    highs = [jnp.where(at_high, pltpu.roll(high_tile, n, 1), 0.0) for n in (8, 72)]
    lows = [jnp.where(at_low, low_tile, 0.0), jnp.where(at_low, pltpu.roll(low_tile, 64, 1), 0.0)]
    for f in range(5):
        c, g = divmod(f, 2)
        edge_face[0, f : f + 1, :] = high_tile[3 + f : 4 + f, :] + highs[g][c : c + 1, :]
        edge_face[1, f : f + 1, :] = low_tile[3 + f : 4 + f, :] + lows[g][c : c + 1, :]
    has_next = jnp.where(place < total - 1, 1.0, 0.0)
    has_prev = jnp.where(place > 0, 1.0, 0.0)
    from_prev = edge_face[0] * has_prev
    from_next = edge_face[1] * has_next
    face = jnp.concatenate(
        [
            jnp.where(left[:8], pltpu.roll(from_prev, 64, 1), from_prev),
            jnp.where(left[:8], from_next, pltpu.roll(from_next, 64, 1)),
        ],
        axis=0,
    )
    slope = mm(side_by_side(face), late[:, SINGLE : SINGLE + 128])
    inner = side_by_side(edge_met[...] * slope + edge_vel[...] * face)
    back = mm(inner, late[:, SINGLE_BACK : SINGLE_BACK + 128]) + mm(
        inner, late[:, SINGLE_BACK + 128 : SINGLE_BACK + 256]
    )
    part = jnp.concatenate([face] * 4, axis=1) * wi_ref[...]
    part = part + jnp.concatenate(
        [
            jnp.where(head16 & left16, back, 0.0),
            jnp.zeros((16, 256), F32),
            jnp.where(head16 | left16, 0.0, back),
        ],
        axis=1,
    )
    ends_ref[...] = part

    for n in range(4):
        face_copy(n).wait_send()
    for n in range(10):
        edge_copy(n).wait_send()


def finish_kernel(local, shared_ref, ends_ref, w_ref, face_met, face_vel, late, out_hbm, res, sem):
    left = lax.broadcasted_iota(jnp.int32, (128, 128), 1) < 64
    shared = [shared_ref[c] for c in range(3)]
    pairs = jnp.concatenate([side_by_side(part) for part in shared], axis=0)
    slopes = mm(pairs, late[:, FORWARD : FORWARD + 256]) + mm(
        pairs, late[:, FORWARD + 256 : FORWARD + 512]
    )
    inners = []
    for f in range(5):
        c, g = divmod(f, 2)
        twice = jnp.where(left == (g == 0), shared[c], pltpu.roll(shared[c], 64, 1))
        slope = slopes[128 * c : 128 * c + 128, 128 * g : 128 * g + 128]
        inners.append(side_by_side(face_met[...] * slope + face_vel[...] * twice))
    inners = jnp.concatenate(inners, axis=0)
    every, lows = [], []
    for at in (0, 256):
        even = mm(pairs, late[:, EXPAND + at : EXPAND + at + 256])
        odd = mm(pairs[:256], late[:, EXPAND + 512 + at : EXPAND + 512 + at + 256])
        every.append((even, odd))
        lows.append(
            mm(inners, late[:, DOWN + at : DOWN + at + 256])
            + mm(inners, late[:, DOWN + 512 + at : DOWN + 512 + at + 256])
        )
    copies = []
    for f in range(5):
        c, g = divmod(f, 2)
        for n, cols in enumerate(HALF):
            spread = every[n][g][128 * c : 128 * c + 128]
            low = lows[n][128 * f : 128 * f + 128]
            res[f, :, cols] = local[f, :, cols] + spread * w_ref[:, cols] + low
        res[f, 0:1, :] = res[f, 0:1, :] + ends_ref[f : f + 1, :]
        res[f, 127:128, :] = res[f, 127:128, :] + ends_ref[8 + f : 9 + f, :]
        copy = pltpu.make_async_copy(res.at[f], out_hbm.at[f], sem.at[f])
        copy.start()
        copies.append(copy)
    for copy in copies:
        copy.wait()


def shards(n_dom, n_sub, adjoint_field, metric, velocity, route, element, code, hanging):
    fields = [jnp.transpose(a, (1, 0, 2)) for a in (adjoint_field, metric, velocity)]
    rows = [a.reshape(1, 128) for a in (route, element, code, hanging)]
    consts = [jnp.asarray(t) for t in tables()]
    operands = [pltpu.with_memory_space_constraint(a, pltpu.HBM) for a in fields + rows + consts]
    made = [
        pltpu.VMEM((5, 128, 512), F32),
        pltpu.VMEM((3, 128, 128), F32),
        pltpu.VMEM((16, 512), F32),
        pltpu.VMEM((128, 512), F32),
        pltpu.VMEM((128, 128), F32),
        pltpu.VMEM((128, 128), F32),
        pltpu.VMEM(consts[4].shape, BF),
    ]
    held = fields + rows + consts[:4] + consts[5:]
    handed = pl.pallas_call(
        functools.partial(kernel, n_dom, n_sub),
        out_shape=made,
        in_specs=[pl.BlockSpec(memory_space=pltpu.HBM)] * len(operands),
        out_specs=[pl.BlockSpec(memory_space=pltpu.VMEM)] * len(made),
        scratch_shapes=[pltpu.VMEM(a.shape, a.dtype) for a in held]
        + [
            pltpu.VMEM((ROWS, 128), BF),
            pltpu.VMEM((4, ROWS, 128), BF),
            pltpu.VMEM((80, 128), F32),
            pltpu.VMEM((80, 128), F32),
            pltpu.VMEM((2, 8, 128), F32),
            pltpu.VMEM((5, 144, 128), F32),
            pltpu.VMEM((5, 144, 128), F32),
            pltpu.VMEM((3, 144, 128), F32),
            pltpu.VMEM((16, 512), F32),
            pltpu.VMEM((16, 128), F32),
            pltpu.VMEM((16, 128), F32),
            pltpu.SemaphoreType.DMA((17,)),
            pltpu.SemaphoreType.DMA((4,)),
            pltpu.SemaphoreType.DMA((4,)),
            pltpu.SemaphoreType.DMA((10,)),
            pltpu.SemaphoreType.DMA((10,)),
        ],
        compiler_params=pltpu.CompilerParams(
            collective_id=0, has_side_effects=True, vmem_limit_bytes=40 << 20
        ),
        name="adjoint",
    )(*operands)
    handed = [pltpu.with_memory_space_constraint(a, pltpu.VMEM) for a in handed]
    result = pl.pallas_call(
        finish_kernel,
        out_shape=jax.ShapeDtypeStruct((5, 128, 512), F32),
        in_specs=[pl.BlockSpec(memory_space=pltpu.VMEM)] * len(handed),
        out_specs=pl.BlockSpec(memory_space=pltpu.HBM),
        scratch_shapes=[pltpu.VMEM((5, 128, 512), F32), pltpu.SemaphoreType.DMA((5,))],
        compiler_params=pltpu.CompilerParams(vmem_limit_bytes=32 << 20),
        name="finish",
    )(*handed)
    return jnp.transpose(result, (1, 0, 2))


def solution(mesh):
    sizes = dict(zip(mesh.axis_names, mesh.devices.shape))
    block = P(("dom", "sub"), None, None)
    flat = P(("dom", "sub"), None)
    return jax.shard_map(
        functools.partial(shards, sizes["dom"], sizes["sub"]),
        mesh=mesh,
        in_specs=(block, block, block, flat, flat, flat, flat),
        out_specs=block,
        check_vma=False,
    )
```

```python
import functools

import jax
import jax.numpy as jnp
import ml_dtypes
import numpy as np
from jax import lax
from jax.experimental import pallas as pl
from jax.experimental.pallas import tpu as pltpu
from jax.sharding import PartitionSpec as P

gll_nodes = np.array(
    [
        -1.0,
        -0.8717401485096066,
        -0.5917001814331423,
        -0.2092992179024789,
        0.2092992179024789,
        0.5917001814331423,
        0.8717401485096066,
        1.0,
    ]
)
viscosity = 0.005
OFFSETS = (-2, -1, 1, 2)
BF = jnp.bfloat16
F32 = jnp.float32


def legendre_seven(points):
    prev = np.ones(points.shape)
    curr = np.array(points)
    for order in range(1, 7):
        nxt = ((2 * order + 1) * points * curr - order * prev) / (order + 1)
        prev, curr = (curr, nxt)
    return curr


def diff_matrix():
    values = legendre_seven(gll_nodes)
    mat = np.zeros((8, 8))
    for row in range(8):
        for col in range(8):
            if row != col:
                mat[row, col] = values[row] / (values[col] * (gll_nodes[row] - gll_nodes[col]))
    mat[0, 0] = -14.0
    mat[7, 7] = 14.0
    return mat


def lagrange_at(points):
    basis = np.ones((8, 8))
    for row in range(8):
        for col in range(8):
            for other in range(8):
                if other != col:
                    basis[row, col] *= (points[row] - gll_nodes[other]) / (
                        gll_nodes[col] - gll_nodes[other]
                    )
    return basis


def split(mat):
    mat = np.asarray(mat, np.float32)
    high = mat.astype(ml_dtypes.bfloat16)
    low = (mat - high.astype(np.float32)).astype(ml_dtypes.bfloat16)
    return np.stack([high, low])


def fold_table():
    parts = [lagrange_at((gll_nodes - 1.0) / 2.0), lagrange_at((gll_nodes + 1.0) / 2.0)]
    turn = np.zeros((64, 64))
    for col in range(64):
        turn[col % 8 * 8 + col // 8, col] = 1.0
    mats = []
    for code in range(8):
        mat = np.kron(parts[code % 2], parts[code // 2 % 2])
        mats.append(mat @ turn if code >= 4 else mat)
    high, low = split(np.stack(mats, axis=1))
    table = np.zeros((2, 2, 8, 8, 8, 64), np.float32)
    for i in range(8):
        a, b = divmod(i, 2)
        rows = slice(8 * i, 8 * i + 8)
        table[0, b, 7 - a] = high[rows].astype(np.float32)
        table[0, b, 3 - a] = high[rows].astype(np.float32)
        table[1, b, 7 - a] = low[rows].astype(np.float32)
    return table.reshape(256, 512).astype(ml_dtypes.bfloat16)


def face_derivatives(dmat):
    eye = np.eye(8)
    return np.kron(dmat, eye).T, np.kron(eye, dmat).T


def to_low_face():
    table = np.zeros((8, 8, 8, 8, 8))
    for i in range(8):
        for k in range(8):
            table[i, k, i, 0, k] = 1.0
    return table.reshape(64, 512)


def tables():
    dmat = diff_matrix().astype(np.float32)
    eye = np.eye(8)
    along_i = np.kron(np.kron(dmat, eye), eye).T
    along_j = np.kron(np.kron(np.eye(4), dmat), eye).T
    along_k = np.kron(np.kron(np.eye(4), eye), dmat).T
    i_tab = split(along_i)
    jk_tab = np.stack([split(along_j), split(along_k)])

    first, second = face_derivatives(dmat)
    both = np.concatenate([first, second], axis=1)
    zero = np.zeros((64, 128))
    high, low = [t.astype(np.float32) for t in split(both)]
    pair_high = np.block([[high, zero], [zero, high]])
    pair_low = np.block([[low, zero], [zero, low]])
    forward = np.stack(
        [np.concatenate([pair_high, pair_high]), np.concatenate([pair_low, 0 * pair_low])]
    )
    single = np.concatenate([high, low, high, 0 * high])
    back = both.T
    spread = to_low_face()
    bh, bl = [t.astype(np.float32) for t in split(back)]
    down = np.stack(
        [np.concatenate([bh, bh]) @ spread, np.concatenate([bl, 0 * bl]) @ spread]
    )
    twice = np.concatenate([np.eye(64), np.eye(64)], axis=1)
    single_back = np.stack(
        [np.concatenate([bh, bh]) @ twice, np.concatenate([bl, 0 * bl]) @ twice]
    )
    every = np.zeros((8, 8, 8, 8, 8))
    for i in range(8):
        for k in range(8):
            every[i, k, i, :, k] = 1.0
    every = every.reshape(64, 512)
    none = np.zeros((64, 512))
    expand = np.stack(
        [
            np.concatenate([every, none, every, none]),
            np.concatenate([none, every, none, every]),
        ]
    )
    gather = spread.T
    blank = np.zeros((512, 64))
    pick = np.concatenate([gather, blank, blank, gather], axis=1)
    cast = lambda t: np.asarray(t, np.float32).astype(ml_dtypes.bfloat16)
    vecs = np.zeros((8, 8, 8, 8), np.float32)
    vecs[0] = dmat[:, 0][None, :, None]
    vecs[1] = dmat[:, 0][:, None, None]
    vecs[2] = dmat[:, 7][:, None, None]
    late = np.concatenate(
        [expand[0], expand[1], down[0], down[1], forward[0], forward[1], single]
        + [single_back[0], single_back[1], np.zeros((256, 128))],
        axis=1,
    )
    return (
        fold_table(),
        i_tab,
        jk_tab,
        cast(pick),
        cast(late),
        vecs.reshape(8, 512),
    )


def halves_of(value):
    high = value.astype(BF)
    low = (value - high.astype(F32)).astype(BF)
    return high, low


def mm(a, b):
    return jnp.dot(a, b, preferred_element_type=F32)


def mmt(a, b):
    return lax.dot_general(a, b, (((1,), (1,)), ((), ())), preferred_element_type=F32)


def side_by_side(value):
    return jnp.concatenate(halves_of(value), axis=1)


ROWS = 336
HALF = [slice(0, 256), slice(256, 512)]
EXPAND, DOWN, FORWARD, SINGLE, SINGLE_BACK = 0, 1024, 2048, 2560, 2688


def apply_operator(x, met, vel, i_tab, jk_tab, out_ref):
    high, low = halves_of(x[...].reshape(640, 512))

    def inner(dim, cols, derived):
        m = met[dim, :, cols] * viscosity
        v = vel[dim, :, cols]
        value = derived.reshape(5, 128, 256) * m[None] + x[:, :, cols] * v[None]
        return halves_of(value.reshape(640, 256))

    parts_i = []
    for cols in HALF:
        derived = jnp.zeros((640, 256), F32)
        for rows in HALF:
            derived += mm(high[:, rows], i_tab[0, rows, cols])
            derived += mm(low[:, rows], i_tab[0, rows, cols])
            derived += mm(high[:, rows], i_tab[1, rows, cols])
        parts_i.append(inner(0, cols, derived))
    for cols in HALF:
        total = jnp.zeros((640, 256), F32)
        for m, rows in enumerate(HALF):
            a, b = parts_i[m]
            total += mmt(a, i_tab[0, cols, rows])
            total += mmt(b, i_tab[0, cols, rows])
            total += mmt(a, i_tab[1, cols, rows])
        for dim in (1, 2):
            derived = mm(high[:, cols], jk_tab[dim - 1, 0])
            derived += mm(low[:, cols], jk_tab[dim - 1, 0])
            derived += mm(high[:, cols], jk_tab[dim - 1, 1])
            a, b = inner(dim, cols, derived)
            total += mmt(a, jk_tab[dim - 1, 0])
            total += mmt(b, jk_tab[dim - 1, 0])
            total += mmt(a, jk_tab[dim - 1, 1])
        out_ref[:, :, cols] = total.reshape(5, 128, 256)


def kernel(n_dom, n_sub, *refs):
    (x_hbm, met_hbm, vel_hbm, route_hbm, elem_hbm, code_hbm, hang_hbm) = refs[:7]
    (fold_hbm, i_hbm, jk_hbm, pick_hbm, late_hbm, vecs_hbm) = refs[7:13]
    (out_ref, shared_ref, ends_ref, w_ref, face_met, face_vel, late) = refs[13:20]
    (wi_ref, edge_met, edge_vel) = refs[20:23]
    (x, met, vel, route_ref, elem_ref, code_ref, hang_ref) = refs[23:30]
    (fold, i_tab, jk_tab, pick, vecs) = refs[30:35]
    (send, got, edge_send, edge_got, low_pad, high_pad, mortar_pad) = refs[35:42]
    (load_sem, send_sem, recv_sem, edge_send_sem, edge_recv_sem) = refs[42:47]

    dom = lax.axis_index("dom")
    sub = lax.axis_index("sub")
    mesh_id = pl.DeviceIdType.MESH
    place = dom * n_sub + sub
    total = n_dom * n_sub

    def along(offset):
        at = dom + offset
        at = jnp.where(at < 0, at + n_dom, at)
        return jnp.where(at >= n_dom, at - n_dom, at)

    peers = [{"dom": along(o), "sub": sub} for o in OFFSETS]
    last, first = sub == n_sub - 1, sub == 0
    sub_up = jnp.where(last, 0, sub + 1)
    sub_down = jnp.where(first, n_sub - 1, sub - 1)
    dom_up = jnp.where(last, 1, 0)
    dom_down = jnp.where(first, -1, 0)
    edge_peers = [{"dom": along(o + dom_up), "sub": sub_up} for o in range(-2, 3)]
    edge_peers += [{"dom": along(o + dom_down), "sub": sub_down} for o in range(-2, 3)]

    loads = []

    def load(src, dst):
        copy = pltpu.make_async_copy(src, dst, load_sem.at[len(loads)])
        copy.start()
        loads.append(copy)
        return copy

    x_loads = [load(x_hbm.at[f], x.at[f]) for f in range(5)]
    first_loads = [
        load(code_hbm, code_ref),
        load(hang_hbm, hang_ref),
        load(route_hbm, route_ref),
        load(elem_hbm, elem_ref),
        load(fold_hbm, fold),
    ]
    barrier = pltpu.get_barrier_semaphore()
    for dev in peers + edge_peers:
        pl.semaphore_signal(barrier, inc=1, device_id=dev, device_id_type=mesh_id)

    lane = lax.broadcasted_iota(jnp.int32, (128, 128), 1)
    row = lax.broadcasted_iota(jnp.int32, (128, 128), 0)
    left = lane < 64
    slot = lax.rem(lane, 64) // 8

    for f in range(5):
        low_pad[f, 136:144, :] = jnp.zeros((8, 128), F32)
        high_pad[f, 0:8, :] = jnp.zeros((8, 128), F32)
    for c in range(3):
        mortar_pad[c, 0:8, :] = jnp.zeros((8, 128), F32)
        mortar_pad[c, 136:144, :] = jnp.zeros((8, 128), F32)

    for copy in first_loads:
        copy.wait()

    def column(ref):
        return jnp.broadcast_to(ref[...].astype(F32), (128, 128)).T

    code = column(code_ref).astype(jnp.int32)
    hang = column(hang_ref)
    odd = lax.rem(code, 2) == 1

    keep = jnp.where(slot == 7, 1.0 - hang, 1.0)
    for copy in x_loads:
        copy.wait()
    later_loads = [
        load(i_hbm, i_tab),
        load(jk_hbm, jk_tab),
        load(met_hbm, met),
        load(vel_hbm, vel),
        load(pick_hbm, pick),
        load(late_hbm, late),
        load(vecs_hbm, vecs),
    ]
    lefts = []
    for f in range(5):
        packed = jnp.where(
            slot == 7,
            x[f, :, 0:128],
            jnp.where(
                slot == 6,
                pltpu.roll(x[f, :, 128:256], 120, 1),
                jnp.where(
                    slot == 5,
                    pltpu.roll(x[f, :, 256:384], 112, 1),
                    pltpu.roll(x[f, :, 384:512], 104, 1),
                ),
            ),
        )
        high = packed.astype(BF)
        low = packed - high.astype(F32)
        mixed = jnp.where(slot >= 4, packed, pltpu.roll(low, 96, 1)).astype(BF)
        lefts.append(jnp.concatenate([mixed, high], axis=1))
    mapped = mm(jnp.concatenate(lefts, axis=0), fold[...])
    faces = []
    for f in range(5):
        one = mapped[128 * f : 128 * f + 128]
        picked = jnp.where(
            code < 4,
            jnp.where(code < 2, one[:, 0:128], one[:, 128:256]),
            jnp.where(code < 6, one[:, 256:384], one[:, 384:512]),
        )
        picked = picked * hang
        other = pltpu.roll(picked, 64, 1)
        faces.append((jnp.where(odd, other, picked), jnp.where(odd, picked, other)))
    pairs = [
        jnp.where(left, faces[0][0], faces[1][1]).astype(BF),
        jnp.where(left, faces[2][0], faces[3][1]).astype(BF),
        faces[4][0].astype(BF),
    ]
    edge_row = lax.broadcasted_iota(jnp.int32, (80, 128), 0)
    tile = edge_row // 8
    part = lax.rem(edge_row, 8)
    wanted_elem = jnp.where(tile < 5, 127, 0)
    wanted_dom = lax.rem(dom + lax.rem(tile, 5) - 2 + n_dom, n_dom)
    chosen = (jnp.broadcast_to(route_ref[...], (80, 128)) == wanted_dom) & (
        jnp.broadcast_to(elem_ref[...], (80, 128)) == wanted_elem
    )
    chosen = jnp.where(chosen, 1.0, 0.0)
    edge_sums = jnp.zeros((80, 128), F32)
    for c in range(3):
        edge_sums += mm(jnp.where(part == c, chosen, 0.0).astype(BF), pairs[c])
    edge_send[...] = edge_sums
    for f in range(5):
        edge_send[19 + f : 20 + f, :] = x[f, 127:128, 384:512] * keep[127:128, :]
        edge_send[59 + f : 60 + f, :] = x[f, 0:1, 0:128] * keep[0:1, :]
    send[0:128, :] = pairs[0]
    send[128:256, :] = pairs[1]
    send[256:320, :] = jnp.where(left[:64], faces[4][0][:64], faces[4][1][64:]).astype(BF)
    meta_row = lax.broadcasted_iota(jnp.int32, (16, 128), 0)
    send[320:336, :] = jnp.where(
        meta_row == 0,
        jnp.broadcast_to(route_ref[...].astype(F32), (16, 128)),
        jnp.broadcast_to(elem_ref[...].astype(F32), (16, 128)),
    ).astype(BF)

    def edge_copy(n):
        rows = pl.ds(8 * n, 8)
        return pltpu.make_async_remote_copy(
            src_ref=edge_send.at[rows],
            dst_ref=edge_got.at[rows],
            send_sem=edge_send_sem.at[n],
            recv_sem=edge_recv_sem.at[n],
            device_id=edge_peers[n],
            device_id_type=mesh_id,
        )

    def face_copy(n):
        return pltpu.make_async_remote_copy(
            src_ref=send,
            dst_ref=got.at[n],
            send_sem=send_sem.at[n],
            recv_sem=recv_sem.at[n],
            device_id=peers[n],
            device_id_type=mesh_id,
        )

    def exchange():
        pl.semaphore_wait(barrier, 14)
        for n in (4, 3, 2, 9, 8, 7):
            edge_copy(n).start()
        for n in (3, 2):
            face_copy(n).start()
        for n in (1, 6, 0, 5):
            edge_copy(n).start()
        for n in (1, 0):
            face_copy(n).start()

    left16 = left[:16]
    head16 = row[:16] < 8

    def alone():
        for f in range(5):
            x[f, :, 128:256] = x[f, :, 128:256] * keep
            x[f, :, 256:384] = x[f, :, 256:384] * keep
            low_pad[f, 8:136, :] = x[f, :, 0:128] * keep
            high_pad[f, 8:136, :] = x[f, :, 384:512] * keep
            above = low_pad[f, 9:137, :]
            below = high_pad[f, 7:135, :]
            x[f, :, 0:128] = low_pad[f, 8:136, :] + jnp.where(left, pltpu.roll(below, 64, 1), 0.0)
            x[f, :, 384:512] = high_pad[f, 8:136, :] + jnp.where(left, 0.0, pltpu.roll(above, 64, 1))
        for copy in later_loads:
            copy.wait()
        apply_operator(x, met, vel, i_tab, jk_tab, out_ref)

        wide = lax.broadcasted_iota(jnp.int32, (128, 512), 1)
        on_low = lax.rem(wide, 64) < 8
        weight = met[1] * viscosity * vecs[0:1, :] + jnp.where(on_low, vel[1], 0.0)
        wh, wl = halves_of(weight)
        for cols in HALF:
            w_ref[:, cols] = (
                mmt(wh[:, cols], jk_tab[0, 0])
                + mmt(wl[:, cols], jk_tab[0, 0])
                + mmt(wh[:, cols], jk_tab[0, 1])
            )

        def low_nodes(src):
            ah, al = halves_of(src[0])
            bh, bl = halves_of(src[2])
            return (
                mm(ah, pick[:, 0:128])
                + mm(al, pick[:, 0:128])
                + mm(bh, pick[:, 128:256])
                + mm(bl, pick[:, 128:256])
            )

        face_met[...] = low_nodes(met) * viscosity
        face_vel[...] = low_nodes(vel)

        edge_rows = lax.broadcasted_iota(jnp.int32, (16, 512), 0)
        edge_wide = lax.broadcasted_iota(jnp.int32, (16, 512), 1)
        head = edge_rows < 8

        def ends(src, dim):
            a = jnp.broadcast_to(src[dim, 0:1, :], (16, 512))
            b = jnp.broadcast_to(src[dim, 127:128, :], (16, 512))
            return a, b

        ma, mb = ends(met, 0)
        va, vb = ends(vel, 0)
        ea = ma * viscosity * vecs[1:2, :] + jnp.where(edge_wide < 64, va, 0.0)
        eb = mb * viscosity * vecs[2:3, :] + jnp.where(edge_wide >= 448, vb, 0.0)
        eh, el = halves_of(jnp.where(head, ea, eb))
        for cols in HALF:
            acc = jnp.zeros((16, 256), F32)
            for rows in HALF:
                acc += mmt(eh[:, rows], i_tab[0, cols, rows])
                acc += mmt(el[:, rows], i_tab[0, cols, rows])
                acc += mmt(eh[:, rows], i_tab[1, cols, rows])
            wi_ref[:, cols] = acc

        def end_faces(src):
            j0, j7 = ends(src, 1)
            k0, k7 = ends(src, 2)
            a = jnp.where(left16, j0[:, 0:128], pltpu.roll(k0[:, 0:128], 64, 1))
            b = jnp.where(left16, pltpu.roll(j7[:, 384:512], 64, 1), k7[:, 384:512])
            return jnp.where(head16, a, b)

        edge_met[...] = end_faces(met) * viscosity
        edge_vel[...] = end_faces(vel)

    column_place = lax.rem(dom, 24)
    early = (column_place < 2) | ((column_place == 2) & (sub == 0))
    turn = jnp.where(early, 0, 1)

    @pl.loop(0, 2)
    def _(step):
        pl.when(step == turn)(alone)
        pl.when(step != turn)(exchange)

    def absorb(sums, blocks):
        hits, firsts, seconds, lasts = [], [], [], []
        for block in blocks:
            route = block[320:321, :].astype(F32)
            elem = block[321:322, :].astype(F32)
            dest = jnp.where(route == dom.astype(F32), elem, -1.0)
            hit = jnp.broadcast_to(dest, (128, 128)) == row.astype(F32)
            hits.append(hit.astype(F32).astype(BF))
            tail = block[256:320, :].astype(F32)
            firsts.append(block[0:128, :])
            seconds.append(block[128:256, :])
            lasts += [jnp.where(left[:64], tail, 0.0), jnp.where(left[:64], 0.0, tail)]
        hits = jnp.concatenate(hits, axis=1)
        return [
            sums[0] + mm(hits, jnp.concatenate(firsts, axis=0)),
            sums[1] + mm(hits, jnp.concatenate(seconds, axis=0)),
            sums[2] + mm(hits, jnp.concatenate(lasts, axis=0).astype(BF)),
        ]

    sums = absorb([jnp.zeros((128, 128), F32)] * 3, [send])
    for pair in ((0, 1), (2, 3)):
        for n in pair:
            face_copy(n).wait_recv()
        sums = absorb(sums, [got.at[n] for n in pair])
    sums[2] = sums[2] + pltpu.roll(sums[2], 64, 1)

    node = lax.rem(lane, 64)
    for c in range(3):
        mortar_pad[c, 8:136, :] = sums[c]
    for c in range(3):
        above = mortar_pad[c, 9:137, :]
        below = mortar_pad[c, 7:135, :]
        shared_ref[c] = (
            sums[c]
            + jnp.where(node >= 56, pltpu.roll(above, 56, 1), 0.0)
            + jnp.where(node < 8, pltpu.roll(below, 72, 1), 0.0)
        )

    for n in range(10):
        edge_copy(n).wait_recv()
    tiles = [edge_got[8 * n : 8 * n + 8, :] for n in range(10)]
    high_tile = tiles[0] + tiles[1] + tiles[2] + tiles[3] + tiles[4]
    low_tile = tiles[5] + tiles[6] + tiles[7] + tiles[8] + tiles[9]
    ends_ref[0:8, :] = high_tile * jnp.where(place > 0, 1.0, 0.0)
    ends_ref[8:16, :] = low_tile * jnp.where(place < total - 1, 1.0, 0.0)

    for n in range(4):
        face_copy(n).wait_send()
    for n in range(10):
        edge_copy(n).wait_send()


def finish_kernel(*refs):
    (local, shared_ref, ends_ref, w_ref, face_met, face_vel, late) = refs[:7]
    (wi_ref, edge_met, edge_vel, out_hbm, res, edge_face, sem) = refs[7:]
    left = lax.broadcasted_iota(jnp.int32, (128, 128), 1) < 64
    lane = lax.broadcasted_iota(jnp.int32, (128, 128), 1)
    left16 = left[:16]
    head16 = lax.broadcasted_iota(jnp.int32, (16, 128), 0) < 8
    edge_face[...] = jnp.zeros((2, 8, 128), F32)
    high_tile, low_tile = ends_ref[0:8, :], ends_ref[8:16, :]
    lane8 = lane[:8]
    at_high = (lane8 >= 64) & (lane8 < 72)
    at_low = lane8 < 8
    highs = [jnp.where(at_high, pltpu.roll(high_tile, n, 1), 0.0) for n in (8, 72)]
    lows = [jnp.where(at_low, low_tile, 0.0), jnp.where(at_low, pltpu.roll(low_tile, 64, 1), 0.0)]
    for f in range(5):
        c, g = divmod(f, 2)
        edge_face[0, f : f + 1, :] = high_tile[3 + f : 4 + f, :] + highs[g][c : c + 1, :]
        edge_face[1, f : f + 1, :] = low_tile[3 + f : 4 + f, :] + lows[g][c : c + 1, :]
    from_prev = edge_face[0]
    from_next = edge_face[1]
    face = jnp.concatenate(
        [
            jnp.where(left[:8], pltpu.roll(from_prev, 64, 1), from_prev),
            jnp.where(left[:8], from_next, pltpu.roll(from_next, 64, 1)),
        ],
        axis=0,
    )
    slope = mm(side_by_side(face), late[:, SINGLE : SINGLE + 128])
    inner = side_by_side(edge_met[...] * slope + edge_vel[...] * face)
    back = mm(inner, late[:, SINGLE_BACK : SINGLE_BACK + 128]) + mm(
        inner, late[:, SINGLE_BACK + 128 : SINGLE_BACK + 256]
    )
    part = jnp.concatenate([face] * 4, axis=1) * wi_ref[...]
    part = part + jnp.concatenate(
        [
            jnp.where(head16 & left16, back, 0.0),
            jnp.zeros((16, 256), F32),
            jnp.where(head16 | left16, 0.0, back),
        ],
        axis=1,
    )
    shared = [shared_ref[c] for c in range(3)]
    pairs = jnp.concatenate([side_by_side(one) for one in shared], axis=0)
    slopes = mm(pairs, late[:, FORWARD : FORWARD + 256]) + mm(
        pairs, late[:, FORWARD + 256 : FORWARD + 512]
    )
    inners = []
    for f in range(5):
        c, g = divmod(f, 2)
        twice = jnp.where(left == (g == 0), shared[c], pltpu.roll(shared[c], 64, 1))
        slope = slopes[128 * c : 128 * c + 128, 128 * g : 128 * g + 128]
        inners.append(side_by_side(face_met[...] * slope + face_vel[...] * twice))
    inners = jnp.concatenate(inners, axis=0)
    every, lows = [], []
    for at in (0, 256):
        even = mm(pairs, late[:, EXPAND + at : EXPAND + at + 256])
        odd = mm(pairs[:256], late[:, EXPAND + 512 + at : EXPAND + 512 + at + 256])
        every.append((even, odd))
        lows.append(
            mm(inners, late[:, DOWN + at : DOWN + at + 256])
            + mm(inners, late[:, DOWN + 512 + at : DOWN + 512 + at + 256])
        )
    copies = []
    for f in range(5):
        c, g = divmod(f, 2)
        for n, cols in enumerate(HALF):
            spread = every[n][g][128 * c : 128 * c + 128]
            low = lows[n][128 * f : 128 * f + 128]
            res[f, :, cols] = local[f, :, cols] + spread * w_ref[:, cols] + low
        res[f, 0:1, :] = res[f, 0:1, :] + part[f : f + 1, :]
        res[f, 127:128, :] = res[f, 127:128, :] + part[8 + f : 9 + f, :]
        copy = pltpu.make_async_copy(res.at[f], out_hbm.at[f], sem.at[f])
        copy.start()
        copies.append(copy)
    for copy in copies:
        copy.wait()


def shards(n_dom, n_sub, adjoint_field, metric, velocity, route, element, code, hanging):
    fields = [jnp.transpose(a, (1, 0, 2)) for a in (adjoint_field, metric, velocity)]
    rows = [a.reshape(1, 128) for a in (route, element, code, hanging)]
    consts = [jnp.asarray(t) for t in tables()]
    operands = [pltpu.with_memory_space_constraint(a, pltpu.HBM) for a in fields + rows + consts]
    made = [
        pltpu.VMEM((5, 128, 512), F32),
        pltpu.VMEM((3, 128, 128), F32),
        pltpu.VMEM((16, 128), F32),
        pltpu.VMEM((128, 512), F32),
        pltpu.VMEM((128, 128), F32),
        pltpu.VMEM((128, 128), F32),
        pltpu.VMEM(consts[4].shape, BF),
        pltpu.VMEM((16, 512), F32),
        pltpu.VMEM((16, 128), F32),
        pltpu.VMEM((16, 128), F32),
    ]
    held = fields + rows + consts[:4] + consts[5:]
    handed = pl.pallas_call(
        functools.partial(kernel, n_dom, n_sub),
        out_shape=made,
        in_specs=[pl.BlockSpec(memory_space=pltpu.HBM)] * len(operands),
        out_specs=[pl.BlockSpec(memory_space=pltpu.VMEM)] * len(made),
        scratch_shapes=[pltpu.VMEM(a.shape, a.dtype) for a in held]
        + [
            pltpu.VMEM((ROWS, 128), BF),
            pltpu.VMEM((4, ROWS, 128), BF),
            pltpu.VMEM((80, 128), F32),
            pltpu.VMEM((80, 128), F32),
            pltpu.VMEM((5, 144, 128), F32),
            pltpu.VMEM((5, 144, 128), F32),
            pltpu.VMEM((3, 144, 128), F32),
            pltpu.SemaphoreType.DMA((17,)),
            pltpu.SemaphoreType.DMA((4,)),
            pltpu.SemaphoreType.DMA((4,)),
            pltpu.SemaphoreType.DMA((10,)),
            pltpu.SemaphoreType.DMA((10,)),
        ],
        compiler_params=pltpu.CompilerParams(
            collective_id=0, has_side_effects=True, vmem_limit_bytes=40 << 20
        ),
        name="adjoint",
    )(*operands)
    handed = [pltpu.with_memory_space_constraint(a, pltpu.VMEM) for a in handed]
    result = pl.pallas_call(
        finish_kernel,
        out_shape=jax.ShapeDtypeStruct((5, 128, 512), F32),
        in_specs=[pl.BlockSpec(memory_space=pltpu.VMEM)] * len(handed),
        out_specs=pl.BlockSpec(memory_space=pltpu.HBM),
        scratch_shapes=[
            pltpu.VMEM((5, 128, 512), F32),
            pltpu.VMEM((2, 8, 128), F32),
            pltpu.SemaphoreType.DMA((5,)),
        ],
        compiler_params=pltpu.CompilerParams(vmem_limit_bytes=32 << 20),
        name="finish",
    )(*handed)
    return jnp.transpose(result, (1, 0, 2))


def solution(mesh):
    sizes = dict(zip(mesh.axis_names, mesh.devices.shape))
    block = P(("dom", "sub"), None, None)
    flat = P(("dom", "sub"), None)
    return jax.shard_map(
        functools.partial(shards, sizes["dom"], sizes["sub"]),
        mesh=mesh,
        in_specs=(block, block, block, flat, flat, flat, flat),
        out_specs=block,
        check_vma=False,
    )
```

```python
import functools

import jax
import jax.numpy as jnp
import ml_dtypes
import numpy as np
from jax import lax
from jax.experimental import pallas as pl
from jax.experimental.pallas import tpu as pltpu
from jax.sharding import PartitionSpec as P

gll_nodes = np.array(
    [
        -1.0,
        -0.8717401485096066,
        -0.5917001814331423,
        -0.2092992179024789,
        0.2092992179024789,
        0.5917001814331423,
        0.8717401485096066,
        1.0,
    ]
)
viscosity = 0.005
OFFSETS = (-2, -1, 1, 2)
BF = jnp.bfloat16
F32 = jnp.float32


def legendre_seven(points):
    prev = np.ones(points.shape)
    curr = np.array(points)
    for order in range(1, 7):
        nxt = ((2 * order + 1) * points * curr - order * prev) / (order + 1)
        prev, curr = (curr, nxt)
    return curr


def diff_matrix():
    values = legendre_seven(gll_nodes)
    mat = np.zeros((8, 8))
    for row in range(8):
        for col in range(8):
            if row != col:
                mat[row, col] = values[row] / (values[col] * (gll_nodes[row] - gll_nodes[col]))
    mat[0, 0] = -14.0
    mat[7, 7] = 14.0
    return mat


def lagrange_at(points):
    basis = np.ones((8, 8))
    for row in range(8):
        for col in range(8):
            for other in range(8):
                if other != col:
                    basis[row, col] *= (points[row] - gll_nodes[other]) / (
                        gll_nodes[col] - gll_nodes[other]
                    )
    return basis


def split(mat):
    mat = np.asarray(mat, np.float32)
    high = mat.astype(ml_dtypes.bfloat16)
    low = (mat - high.astype(np.float32)).astype(ml_dtypes.bfloat16)
    return np.stack([high, low])


def fold_table():
    parts = [lagrange_at((gll_nodes - 1.0) / 2.0), lagrange_at((gll_nodes + 1.0) / 2.0)]
    turn = np.zeros((64, 64))
    for col in range(64):
        turn[col % 8 * 8 + col // 8, col] = 1.0
    mats = []
    for code in range(8):
        mat = np.kron(parts[code % 2], parts[code // 2 % 2])
        mats.append(mat @ turn if code >= 4 else mat)
    high, low = split(np.stack(mats, axis=1))
    table = np.zeros((2, 2, 8, 8, 8, 64), np.float32)
    for i in range(8):
        a, b = divmod(i, 2)
        rows = slice(8 * i, 8 * i + 8)
        table[0, b, 7 - a] = high[rows].astype(np.float32)
        table[0, b, 3 - a] = high[rows].astype(np.float32)
        table[1, b, 7 - a] = low[rows].astype(np.float32)
    return table.reshape(256, 512).astype(ml_dtypes.bfloat16)


def face_derivatives(dmat):
    eye = np.eye(8)
    return np.kron(dmat, eye).T, np.kron(eye, dmat).T


def to_low_face():
    table = np.zeros((8, 8, 8, 8, 8))
    for i in range(8):
        for k in range(8):
            table[i, k, i, 0, k] = 1.0
    return table.reshape(64, 512)


def tables():
    dmat = diff_matrix().astype(np.float32)
    eye = np.eye(8)
    along_i = np.kron(np.kron(dmat, eye), eye).T
    along_j = np.kron(np.kron(np.eye(4), dmat), eye).T
    along_k = np.kron(np.kron(np.eye(4), eye), dmat).T
    i_tab = split(along_i)
    jk_tab = np.stack([split(along_j), split(along_k)])

    first, second = face_derivatives(dmat)
    both = np.concatenate([first, second], axis=1)
    zero = np.zeros((64, 128))
    high, low = [t.astype(np.float32) for t in split(both)]
    pair_high = np.block([[high, zero], [zero, high]])
    pair_low = np.block([[low, zero], [zero, low]])
    forward = np.stack(
        [np.concatenate([pair_high, pair_high]), np.concatenate([pair_low, 0 * pair_low])]
    )
    single = np.concatenate([high, low, high, 0 * high])
    back = both.T
    spread = to_low_face()
    bh, bl = [t.astype(np.float32) for t in split(back)]
    down = np.stack(
        [np.concatenate([bh, bh]) @ spread, np.concatenate([bl, 0 * bl]) @ spread]
    )
    twice = np.concatenate([np.eye(64), np.eye(64)], axis=1)
    single_back = np.stack(
        [np.concatenate([bh, bh]) @ twice, np.concatenate([bl, 0 * bl]) @ twice]
    )
    every = np.zeros((8, 8, 8, 8, 8))
    for i in range(8):
        for k in range(8):
            every[i, k, i, :, k] = 1.0
    every = every.reshape(64, 512)
    none = np.zeros((64, 512))
    expand = np.stack(
        [
            np.concatenate([every, none, every, none]),
            np.concatenate([none, every, none, every]),
        ]
    )
    gather = spread.T
    blank = np.zeros((512, 64))
    pick = np.concatenate([gather, blank, blank, gather], axis=1)
    cast = lambda t: np.asarray(t, np.float32).astype(ml_dtypes.bfloat16)
    vecs = np.zeros((8, 8, 8, 8), np.float32)
    vecs[0] = dmat[:, 0][None, :, None]
    vecs[1] = dmat[:, 0][:, None, None]
    vecs[2] = dmat[:, 7][:, None, None]
    late = np.concatenate(
        [expand[0], expand[1], down[0], down[1], forward[0], forward[1], single]
        + [single_back[0], single_back[1], np.zeros((256, 128))],
        axis=1,
    )
    return (
        fold_table(),
        i_tab,
        jk_tab,
        cast(pick),
        cast(late),
        vecs.reshape(8, 512),
    )


def halves_of(value):
    high = value.astype(BF)
    low = (value - high.astype(F32)).astype(BF)
    return high, low


def mm(a, b):
    return jnp.dot(a, b, preferred_element_type=F32)


def mmt(a, b):
    return lax.dot_general(a, b, (((1,), (1,)), ((), ())), preferred_element_type=F32)


def side_by_side(value):
    return jnp.concatenate(halves_of(value), axis=1)


ROWS = 336
HALF = [slice(0, 256), slice(256, 512)]
EXPAND, DOWN, FORWARD, SINGLE, SINGLE_BACK = 0, 1024, 2048, 2560, 2688


def apply_operator(x, met, vel, i_tab, jk_tab, out_ref):
    high, low = halves_of(x[...].reshape(640, 512))

    def inner(dim, cols, derived):
        m = met[dim, :, cols] * viscosity
        v = vel[dim, :, cols]
        value = derived.reshape(5, 128, 256) * m[None] + x[:, :, cols] * v[None]
        return halves_of(value.reshape(640, 256))

    parts_i = []
    for cols in HALF:
        derived = jnp.zeros((640, 256), F32)
        for rows in HALF:
            derived += mm(high[:, rows], i_tab[0, rows, cols])
            derived += mm(low[:, rows], i_tab[0, rows, cols])
            derived += mm(high[:, rows], i_tab[1, rows, cols])
        parts_i.append(inner(0, cols, derived))
    for cols in HALF:
        total = jnp.zeros((640, 256), F32)
        for m, rows in enumerate(HALF):
            a, b = parts_i[m]
            total += mmt(a, i_tab[0, cols, rows])
            total += mmt(b, i_tab[0, cols, rows])
            total += mmt(a, i_tab[1, cols, rows])
        for dim in (1, 2):
            derived = mm(high[:, cols], jk_tab[dim - 1, 0])
            derived += mm(low[:, cols], jk_tab[dim - 1, 0])
            derived += mm(high[:, cols], jk_tab[dim - 1, 1])
            a, b = inner(dim, cols, derived)
            total += mmt(a, jk_tab[dim - 1, 0])
            total += mmt(b, jk_tab[dim - 1, 0])
            total += mmt(a, jk_tab[dim - 1, 1])
        out_ref[:, :, cols] = total.reshape(5, 128, 256)


def finish(res, shared_ref, w_ref, face_met, face_vel, late):
    left = lax.broadcasted_iota(jnp.int32, (128, 128), 1) < 64
    shared = [shared_ref[c] for c in range(3)]
    pairs = jnp.concatenate([side_by_side(part) for part in shared], axis=0)
    slopes = mm(pairs, late[:, FORWARD : FORWARD + 256]) + mm(
        pairs, late[:, FORWARD + 256 : FORWARD + 512]
    )
    inners = []
    for f in range(5):
        c, g = divmod(f, 2)
        twice = jnp.where(left == (g == 0), shared[c], pltpu.roll(shared[c], 64, 1))
        slope = slopes[128 * c : 128 * c + 128, 128 * g : 128 * g + 128]
        inners.append(side_by_side(face_met[...] * slope + face_vel[...] * twice))
    inners = jnp.concatenate(inners, axis=0)
    every, lows = [], []
    for at in (0, 256):
        even = mm(pairs, late[:, EXPAND + at : EXPAND + at + 256])
        odd = mm(pairs[:256], late[:, EXPAND + 512 + at : EXPAND + 512 + at + 256])
        every.append((even, odd))
        lows.append(
            mm(inners, late[:, DOWN + at : DOWN + at + 256])
            + mm(inners, late[:, DOWN + 512 + at : DOWN + 512 + at + 256])
        )
    for f in range(5):
        c, g = divmod(f, 2)
        for n, cols in enumerate(HALF):
            spread = every[n][g][128 * c : 128 * c + 128]
            low = lows[n][128 * f : 128 * f + 128]
            res[f, :, cols] = res[f, :, cols] + spread * w_ref[:, cols] + low


def kernel(n_dom, n_sub, *refs):
    (x_hbm, met_hbm, vel_hbm, route_hbm, elem_hbm, code_hbm, hang_hbm) = refs[:7]
    (fold_hbm, i_hbm, jk_hbm, pick_hbm, late_hbm, vecs_hbm) = refs[7:13]
    (out_ref, shared_ref, w_ref, face_met, face_vel, late) = refs[13:19]
    (x, met, vel, route_ref, elem_ref, code_ref, hang_ref) = refs[19:26]
    (fold, i_tab, jk_tab, pick, vecs) = refs[26:31]
    (send, got, edge_send, edge_got, edge_face, low_pad, high_pad, mortar_pad) = refs[31:39]
    (wi_ref, edge_met, edge_vel) = refs[39:42]
    (load_sem, send_sem, recv_sem, edge_send_sem, edge_recv_sem) = refs[42:47]

    dom = lax.axis_index("dom")
    sub = lax.axis_index("sub")
    mesh_id = pl.DeviceIdType.MESH
    place = dom * n_sub + sub
    total = n_dom * n_sub

    def along(offset):
        at = dom + offset
        at = jnp.where(at < 0, at + n_dom, at)
        return jnp.where(at >= n_dom, at - n_dom, at)

    peers = [{"dom": along(o), "sub": sub} for o in OFFSETS]
    last, first = sub == n_sub - 1, sub == 0
    sub_up = jnp.where(last, 0, sub + 1)
    sub_down = jnp.where(first, n_sub - 1, sub - 1)
    dom_up = jnp.where(last, 1, 0)
    dom_down = jnp.where(first, -1, 0)
    edge_peers = [{"dom": along(o + dom_up), "sub": sub_up} for o in range(-2, 3)]
    edge_peers += [{"dom": along(o + dom_down), "sub": sub_down} for o in range(-2, 3)]

    loads = []

    def load(src, dst):
        copy = pltpu.make_async_copy(src, dst, load_sem.at[len(loads)])
        copy.start()
        loads.append(copy)
        return copy

    x_loads = [load(x_hbm.at[f], x.at[f]) for f in range(5)]
    first_loads = [
        load(code_hbm, code_ref),
        load(hang_hbm, hang_ref),
        load(route_hbm, route_ref),
        load(elem_hbm, elem_ref),
        load(fold_hbm, fold),
    ]
    barrier = pltpu.get_barrier_semaphore()
    for dev in peers + edge_peers:
        pl.semaphore_signal(barrier, inc=1, device_id=dev, device_id_type=mesh_id)

    lane = lax.broadcasted_iota(jnp.int32, (128, 128), 1)
    row = lax.broadcasted_iota(jnp.int32, (128, 128), 0)
    left = lane < 64
    slot = lax.rem(lane, 64) // 8

    for f in range(5):
        low_pad[f, 136:144, :] = jnp.zeros((8, 128), F32)
        high_pad[f, 0:8, :] = jnp.zeros((8, 128), F32)
    edge_face[...] = jnp.zeros((2, 8, 128), F32)
    for c in range(3):
        mortar_pad[c, 0:8, :] = jnp.zeros((8, 128), F32)
        mortar_pad[c, 136:144, :] = jnp.zeros((8, 128), F32)

    for copy in first_loads:
        copy.wait()

    def column(ref):
        return jnp.broadcast_to(ref[...].astype(F32), (128, 128)).T

    code = column(code_ref).astype(jnp.int32)
    hang = column(hang_ref)
    odd = lax.rem(code, 2) == 1

    keep = jnp.where(slot == 7, 1.0 - hang, 1.0)
    for copy in x_loads:
        copy.wait()
    later_loads = [
        load(i_hbm, i_tab),
        load(jk_hbm, jk_tab),
        load(met_hbm, met),
        load(vel_hbm, vel),
        load(pick_hbm, pick),
        load(late_hbm, late),
        load(vecs_hbm, vecs),
    ]
    lefts = []
    for f in range(5):
        packed = jnp.where(
            slot == 7,
            x[f, :, 0:128],
            jnp.where(
                slot == 6,
                pltpu.roll(x[f, :, 128:256], 120, 1),
                jnp.where(
                    slot == 5,
                    pltpu.roll(x[f, :, 256:384], 112, 1),
                    pltpu.roll(x[f, :, 384:512], 104, 1),
                ),
            ),
        )
        high = packed.astype(BF)
        low = packed - high.astype(F32)
        mixed = jnp.where(slot >= 4, packed, pltpu.roll(low, 96, 1)).astype(BF)
        lefts.append(jnp.concatenate([mixed, high], axis=1))
    mapped = mm(jnp.concatenate(lefts, axis=0), fold[...])
    faces = []
    for f in range(5):
        one = mapped[128 * f : 128 * f + 128]
        picked = jnp.where(
            code < 4,
            jnp.where(code < 2, one[:, 0:128], one[:, 128:256]),
            jnp.where(code < 6, one[:, 256:384], one[:, 384:512]),
        )
        picked = picked * hang
        other = pltpu.roll(picked, 64, 1)
        faces.append((jnp.where(odd, other, picked), jnp.where(odd, picked, other)))
    pairs = [
        jnp.where(left, faces[0][0], faces[1][1]).astype(BF),
        jnp.where(left, faces[2][0], faces[3][1]).astype(BF),
        faces[4][0].astype(BF),
    ]
    edge_row = lax.broadcasted_iota(jnp.int32, (80, 128), 0)
    tile = edge_row // 8
    part = lax.rem(edge_row, 8)
    wanted_elem = jnp.where(tile < 5, 127, 0)
    wanted_dom = lax.rem(dom + lax.rem(tile, 5) - 2 + n_dom, n_dom)
    chosen = (jnp.broadcast_to(route_ref[...], (80, 128)) == wanted_dom) & (
        jnp.broadcast_to(elem_ref[...], (80, 128)) == wanted_elem
    )
    chosen = jnp.where(chosen, 1.0, 0.0)
    edge_sums = jnp.zeros((80, 128), F32)
    for c in range(3):
        edge_sums += mm(jnp.where(part == c, chosen, 0.0).astype(BF), pairs[c])
    edge_send[...] = edge_sums
    for f in range(5):
        edge_send[19 + f : 20 + f, :] = x[f, 127:128, 384:512] * keep[127:128, :]
        edge_send[59 + f : 60 + f, :] = x[f, 0:1, 0:128] * keep[0:1, :]
    send[0:128, :] = pairs[0]
    send[128:256, :] = pairs[1]
    send[256:320, :] = jnp.where(left[:64], faces[4][0][:64], faces[4][1][64:]).astype(BF)
    meta_row = lax.broadcasted_iota(jnp.int32, (16, 128), 0)
    send[320:336, :] = jnp.where(
        meta_row == 0,
        jnp.broadcast_to(route_ref[...].astype(F32), (16, 128)),
        jnp.broadcast_to(elem_ref[...].astype(F32), (16, 128)),
    ).astype(BF)

    def edge_copy(n):
        rows = pl.ds(8 * n, 8)
        return pltpu.make_async_remote_copy(
            src_ref=edge_send.at[rows],
            dst_ref=edge_got.at[rows],
            send_sem=edge_send_sem.at[n],
            recv_sem=edge_recv_sem.at[n],
            device_id=edge_peers[n],
            device_id_type=mesh_id,
        )

    def face_copy(n):
        return pltpu.make_async_remote_copy(
            src_ref=send,
            dst_ref=got.at[n],
            send_sem=send_sem.at[n],
            recv_sem=recv_sem.at[n],
            device_id=peers[n],
            device_id_type=mesh_id,
        )

    def exchange():
        pl.semaphore_wait(barrier, 14)
        for n in (4, 9, 3, 8):
            edge_copy(n).start()
        for n in (3, 2):
            face_copy(n).start()
        for n in (2, 7, 1, 6, 0, 5):
            edge_copy(n).start()
        for n in (1, 0):
            face_copy(n).start()

    left16 = left[:16]
    head16 = row[:16] < 8

    def alone():
        for f in range(5):
            x[f, :, 128:256] = x[f, :, 128:256] * keep
            x[f, :, 256:384] = x[f, :, 256:384] * keep
            low_pad[f, 8:136, :] = x[f, :, 0:128] * keep
            high_pad[f, 8:136, :] = x[f, :, 384:512] * keep
            above = low_pad[f, 9:137, :]
            below = high_pad[f, 7:135, :]
            x[f, :, 0:128] = low_pad[f, 8:136, :] + jnp.where(left, pltpu.roll(below, 64, 1), 0.0)
            x[f, :, 384:512] = high_pad[f, 8:136, :] + jnp.where(left, 0.0, pltpu.roll(above, 64, 1))
        for copy in later_loads:
            copy.wait()
        apply_operator(x, met, vel, i_tab, jk_tab, out_ref)

        wide = lax.broadcasted_iota(jnp.int32, (128, 512), 1)
        on_low = lax.rem(wide, 64) < 8
        weight = met[1] * viscosity * vecs[0:1, :] + jnp.where(on_low, vel[1], 0.0)
        wh, wl = halves_of(weight)
        for cols in HALF:
            w_ref[:, cols] = (
                mmt(wh[:, cols], jk_tab[0, 0])
                + mmt(wl[:, cols], jk_tab[0, 0])
                + mmt(wh[:, cols], jk_tab[0, 1])
            )

        def low_nodes(src):
            ah, al = halves_of(src[0])
            bh, bl = halves_of(src[2])
            return (
                mm(ah, pick[:, 0:128])
                + mm(al, pick[:, 0:128])
                + mm(bh, pick[:, 128:256])
                + mm(bl, pick[:, 128:256])
            )

        face_met[...] = low_nodes(met) * viscosity
        face_vel[...] = low_nodes(vel)

        edge_rows = lax.broadcasted_iota(jnp.int32, (16, 512), 0)
        edge_wide = lax.broadcasted_iota(jnp.int32, (16, 512), 1)
        head = edge_rows < 8

        def ends(src, dim):
            a = jnp.broadcast_to(src[dim, 0:1, :], (16, 512))
            b = jnp.broadcast_to(src[dim, 127:128, :], (16, 512))
            return a, b

        ma, mb = ends(met, 0)
        va, vb = ends(vel, 0)
        ea = ma * viscosity * vecs[1:2, :] + jnp.where(edge_wide < 64, va, 0.0)
        eb = mb * viscosity * vecs[2:3, :] + jnp.where(edge_wide >= 448, vb, 0.0)
        eh, el = halves_of(jnp.where(head, ea, eb))
        for cols in HALF:
            acc = jnp.zeros((16, 256), F32)
            for rows in HALF:
                acc += mmt(eh[:, rows], i_tab[0, cols, rows])
                acc += mmt(el[:, rows], i_tab[0, cols, rows])
                acc += mmt(eh[:, rows], i_tab[1, cols, rows])
            wi_ref[:, cols] = acc

        def end_faces(src):
            j0, j7 = ends(src, 1)
            k0, k7 = ends(src, 2)
            a = jnp.where(left16, j0[:, 0:128], pltpu.roll(k0[:, 0:128], 64, 1))
            b = jnp.where(left16, pltpu.roll(j7[:, 384:512], 64, 1), k7[:, 384:512])
            return jnp.where(head16, a, b)

        edge_met[...] = end_faces(met) * viscosity
        edge_vel[...] = end_faces(vel)

    column_place = lax.rem(dom, 24)
    early = (column_place < 2) | ((column_place == 2) & (sub == 0))
    turn = jnp.where(early, 0, 1)

    @pl.loop(0, 2)
    def _(step):
        pl.when(step == turn)(alone)
        pl.when(step != turn)(exchange)

    def absorb(sums, block):
        route = block[320:321, :].astype(F32)
        elem = block[321:322, :].astype(F32)
        dest = jnp.where(route == dom.astype(F32), elem, -1.0)
        hit = (jnp.broadcast_to(dest, (128, 128)) == row.astype(F32)).astype(F32).astype(BF)
        tail = block[256:320, :].astype(F32)
        last = jnp.concatenate(
            [jnp.where(left[:64], tail, 0.0), jnp.where(left[:64], 0.0, tail)], axis=0
        ).astype(BF)
        return [
            sums[0] + mm(hit, block[0:128, :]),
            sums[1] + mm(hit, block[128:256, :]),
            sums[2] + mm(hit, last),
        ]

    sums = absorb([jnp.zeros((128, 128), F32)] * 3, send)
    for n in (0, 1, 2, 3):
        face_copy(n).wait_recv()
        sums = absorb(sums, got.at[n])
    sums[2] = sums[2] + pltpu.roll(sums[2], 64, 1)

    node = lax.rem(lane, 64)
    for c in range(3):
        mortar_pad[c, 8:136, :] = sums[c]
    for c in range(3):
        above = mortar_pad[c, 9:137, :]
        below = mortar_pad[c, 7:135, :]
        shared_ref[c] = (
            sums[c]
            + jnp.where(node >= 56, pltpu.roll(above, 56, 1), 0.0)
            + jnp.where(node < 8, pltpu.roll(below, 72, 1), 0.0)
        )

    finish(out_ref, shared_ref, w_ref, face_met, face_vel, late)

    for n in range(10):
        edge_copy(n).wait_recv()
    tiles = [edge_got[8 * n : 8 * n + 8, :] for n in range(10)]
    high_tile = tiles[0] + tiles[1] + tiles[2] + tiles[3] + tiles[4]
    low_tile = tiles[5] + tiles[6] + tiles[7] + tiles[8] + tiles[9]
    lane8 = lane[:8]
    at_high = (lane8 >= 64) & (lane8 < 72)
    at_low = lane8 < 8
    highs = [jnp.where(at_high, pltpu.roll(high_tile, n, 1), 0.0) for n in (8, 72)]
    lows = [jnp.where(at_low, low_tile, 0.0), jnp.where(at_low, pltpu.roll(low_tile, 64, 1), 0.0)]
    for f in range(5):
        c, g = divmod(f, 2)
        edge_face[0, f : f + 1, :] = high_tile[3 + f : 4 + f, :] + highs[g][c : c + 1, :]
        edge_face[1, f : f + 1, :] = low_tile[3 + f : 4 + f, :] + lows[g][c : c + 1, :]
    has_next = jnp.where(place < total - 1, 1.0, 0.0)
    has_prev = jnp.where(place > 0, 1.0, 0.0)
    from_prev = edge_face[0] * has_prev
    from_next = edge_face[1] * has_next
    face = jnp.concatenate(
        [
            jnp.where(left[:8], pltpu.roll(from_prev, 64, 1), from_prev),
            jnp.where(left[:8], from_next, pltpu.roll(from_next, 64, 1)),
        ],
        axis=0,
    )
    slope = mm(side_by_side(face), late[:, SINGLE : SINGLE + 128])
    inner = side_by_side(edge_met[...] * slope + edge_vel[...] * face)
    back = mm(inner, late[:, SINGLE_BACK : SINGLE_BACK + 128]) + mm(
        inner, late[:, SINGLE_BACK + 128 : SINGLE_BACK + 256]
    )
    part = jnp.concatenate([face] * 4, axis=1) * wi_ref[...]
    part = part + jnp.concatenate(
        [
            jnp.where(head16 & left16, back, 0.0),
            jnp.zeros((16, 256), F32),
            jnp.where(head16 | left16, 0.0, back),
        ],
        axis=1,
    )
    for f in range(5):
        out_ref[f, 0:1, :] = out_ref[f, 0:1, :] + part[f : f + 1, :]
        out_ref[f, 127:128, :] = out_ref[f, 127:128, :] + part[8 + f : 9 + f, :]

    for n in range(4):
        face_copy(n).wait_send()
    for n in range(10):
        edge_copy(n).wait_send()


def shards(n_dom, n_sub, adjoint_field, metric, velocity, route, element, code, hanging):
    fields = [jnp.transpose(a, (1, 0, 2)) for a in (adjoint_field, metric, velocity)]
    rows = [a.reshape(1, 128) for a in (route, element, code, hanging)]
    consts = [jnp.asarray(t) for t in tables()]
    operands = [pltpu.with_memory_space_constraint(a, pltpu.HBM) for a in fields + rows + consts]
    made = [
        pltpu.VMEM((3, 128, 128), F32),
        pltpu.VMEM((128, 512), F32),
        pltpu.VMEM((128, 128), F32),
        pltpu.VMEM((128, 128), F32),
        pltpu.VMEM(consts[4].shape, BF),
    ]
    held = fields + rows + consts[:4] + consts[5:]
    result = pl.pallas_call(
        functools.partial(kernel, n_dom, n_sub),
        out_shape=pltpu.VMEM((5, 128, 512), F32),
        in_specs=[pl.BlockSpec(memory_space=pltpu.HBM)] * len(operands),
        out_specs=pl.BlockSpec(memory_space=pltpu.VMEM),
        scratch_shapes=made + [pltpu.VMEM(a.shape, a.dtype) for a in held]
        + [
            pltpu.VMEM((ROWS, 128), BF),
            pltpu.VMEM((4, ROWS, 128), BF),
            pltpu.VMEM((80, 128), F32),
            pltpu.VMEM((80, 128), F32),
            pltpu.VMEM((2, 8, 128), F32),
            pltpu.VMEM((5, 144, 128), F32),
            pltpu.VMEM((5, 144, 128), F32),
            pltpu.VMEM((3, 144, 128), F32),
            pltpu.VMEM((16, 512), F32),
            pltpu.VMEM((16, 128), F32),
            pltpu.VMEM((16, 128), F32),
            pltpu.SemaphoreType.DMA((17,)),
            pltpu.SemaphoreType.DMA((4,)),
            pltpu.SemaphoreType.DMA((4,)),
            pltpu.SemaphoreType.DMA((10,)),
            pltpu.SemaphoreType.DMA((10,)),
        ],
        compiler_params=pltpu.CompilerParams(
            collective_id=0, has_side_effects=True, vmem_limit_bytes=40 << 20
        ),
        name="adjoint",
    )(*operands)
    return jnp.transpose(result, (1, 0, 2))


def solution(mesh):
    sizes = dict(zip(mesh.axis_names, mesh.devices.shape))
    block = P(("dom", "sub"), None, None)
    flat = P(("dom", "sub"), None)
    return jax.shard_map(
        functools.partial(shards, sizes["dom"], sizes["sub"]),
        mesh=mesh,
        in_specs=(block, block, block, flat, flat, flat, flat),
        out_specs=block,
        check_vma=False,
    )
```
